256 devices in a mesh: mem: 32 (over z, x), lon: 4 (over y), lat: 2 (over core).
Axes of the slice: x: 4, y: 4, z: 8, core: 2. Of those that a mesh axis runs over, the one named last changes fastest.
Arguments:
- ens_obs: bfloat16 [1024, 8, 16, 128], P('mem', 'lat', 'lon'), may hold values from -16 to 16
- innovation: bfloat16 [8, 16, 128], P('lat', 'lon'), may hold values from -6 to 6
- obs_weight: bfloat16 [8, 16, 128], P('lat', 'lon'), may hold values from 0.5 to 5
- loc_list: int32 [32, 8, 4], P(None, ('lon', 'lat')), may hold values from 0 to 47, as said below
- counts: int32 [32, 8], P('mem', ('lon', 'lat')), may hold values from 1 to 4, as said below
- taper: float32 [32, 8, 4], P('mem', ('lon', 'lat')), may hold values from 0.2 to 1
- state: bfloat16 [1024, 32, 8, 1280], P('mem', None, ('lon', 'lat')), may hold values from -6 to 6
Outputs:
- analysis: bfloat16 [1024, 32, 8, 1280], P('mem', None, ('lon', 'lat'))
The draws below stay inside these ranges and needn't reach their ends.
Inputs may be any that keep to these rules, and one draw needn't show every extreme that they name: `loc_list`: the 4 entries of a patch name different window blocks; only the first counts entries are used. `counts`: some patch uses all 4 listed blocks in every draw.
All inputs are finite; a program needn't handle non-finite values.
Results may differ from the reference program's by a relative error of at most 0.0068.
Values may be sent and summed in bfloat16 or wider, within the bound.
A program may use at most 64 MiB of HBM per device.

```python
import math
import jax
import jax.numpy as jnp
from jax import lax

MEMBERS = 1024
OBS_BLK = 128
LMAX = 4
BLT = 4
BLN = 4
NSI = 2
P_GRP = 32
GROUPS = 8
NBLAT = 8
NBLON = 16
NWIN = 48
SDIM = 1280
N_LAT = 2


def draw_ens_obs(key, part):
    key_base = jax.random.fold_in(key, 11)
    key_member = jax.random.fold_in(key, 12)
    key_column = jax.random.fold_in(key, 13)
    full_shape = (MEMBERS, NBLAT, NBLON, OBS_BLK)
    base_draw = jnp.clip(jax.random.normal(key_base, full_shape, jnp.float32), -4.0, 4.0)
    member_scale = jnp.exp(jax.random.uniform(key_member, (MEMBERS, 1, 1, 1), jnp.float32, -0.693, 0.693))
    obs_scale = jnp.exp(jax.random.uniform(key_column, (1, NBLAT, NBLON, OBS_BLK), jnp.float32, -0.693, 0.693))
    return (base_draw * member_scale * obs_scale).astype(jnp.bfloat16)


def draw_loc_list(key, part):
    patch_keys = jax.random.split(jax.random.fold_in(key, 21), P_GRP * GROUPS)
    orders = jax.vmap(lambda single_key: jax.random.permutation(single_key, NWIN))(patch_keys)
    return orders[:, :LMAX].reshape(P_GRP, GROUPS, LMAX).astype(jnp.int32)


def draw_counts(key, part):
    flat_counts = jax.random.randint(jax.random.fold_in(key, 31), (P_GRP * GROUPS,), 1, LMAX + 1)
    forced_pos = jax.random.randint(jax.random.fold_in(key, 32), (), 0, P_GRP * GROUPS)
    flat_counts = flat_counts.at[forced_pos].set(LMAX)
    return flat_counts.reshape(P_GRP, GROUPS).astype(jnp.int32)


def block_scale(stream_key, shape, cuts, least, high):
    level = 1.0
    for position, parts in cuts:
        steps = jax.random.uniform(jax.random.fold_in(jax.random.fold_in(stream_key, 6), position), (parts,), jnp.float32, least / len(cuts), high / len(cuts))
        level = level * jnp.repeat(jnp.exp(steps), shape[position] // parts).reshape((-1,) + (1,) * (len(shape) - 1 - position))
    return level


def centred(own_key, shape, spread, limit, cuts=(), kind=jnp.bfloat16):
    values = spread * jax.random.normal(own_key, shape, jnp.float32)
    if cuts:
        values = values * block_scale(own_key, shape, cuts, -0.22, 0.18)
    return jnp.clip(values, -limit, limit).astype(kind)


def setup_inputs(seed: int = 0) -> dict:
    key_list = jax.random.split(jax.random.key(seed), 8)
    ens_obs = draw_ens_obs(jax.random.fold_in(key_list[7], 71), 0)
    innovation = centred(key_list[1], (NBLAT, NBLON, OBS_BLK), 1.0, 6.0, ((0, 2), (1, 4)))
    obs_weight = jnp.clip(jnp.exp(math.log(5.0) - 2.3025851 * jax.random.uniform(key_list[2], (NBLAT, NBLON, OBS_BLK), jnp.float32) ** block_scale(key_list[2], (NBLAT, NBLON, OBS_BLK), ((0, 2), (1, 4)), -0.2, 0.2)), 0.5, 5.0).astype(jnp.bfloat16)
    loc_list = draw_loc_list(jax.random.fold_in(key_list[7], 71), 0)
    counts = draw_counts(jax.random.fold_in(key_list[7], 71), 0)
    taper = jnp.clip(jnp.exp(math.log(1.0) - 1.609438 * jax.random.uniform(key_list[5], (P_GRP, GROUPS, LMAX), jnp.float32) ** block_scale(key_list[5], (P_GRP, GROUPS, LMAX), ((0, 32), (1, 8)), -0.2, 0.2)), 0.2, 1.0)
    state = centred(key_list[6], (MEMBERS, P_GRP, GROUPS, SDIM), 1.0, 6.0, ((0, 32), (2, 8)))
    return {"ens_obs": ens_obs, "innovation": innovation, "obs_weight": obs_weight, "loc_list": loc_list, "counts": counts, "taper": taper, "state": state}


def inverse_root(start_low):
    member_total = start_low.shape[0]
    identity = jnp.eye(member_total, dtype=jnp.float32)
    upper_iter = start_low
    lower_iter = start_low
    for sweep_index in range(NSI):
        if sweep_index == 0:
            product = start_low.astype(jnp.float32)
        else:
            product = jnp.dot(lower_iter, upper_iter, preferred_element_type=jnp.float32)
        halfstep = 0.5 * (3.0 * identity - product)
        half_low = halfstep.astype(jnp.bfloat16)
        if sweep_index == NSI - 1:
            return jnp.dot(half_low, lower_iter, preferred_element_type=jnp.float32)
        next_upper = jnp.dot(upper_iter, half_low, preferred_element_type=jnp.float32).astype(jnp.bfloat16)
        if sweep_index == 0:
            lower_iter = half_low
        else:
            lower_iter = jnp.dot(half_low, lower_iter, preferred_element_type=jnp.float32).astype(jnp.bfloat16)
        upper_iter = next_upper

def weights_from_gram(gram_mat, drive_vec):
    member_total = gram_mat.shape[0]
    divisor = float(member_total - 1)
    identity = jnp.eye(member_total, dtype=jnp.float32)
    a_matrix = identity + gram_mat / divisor
    trace_level = 2.0 * jnp.trace(a_matrix) / member_total
    start_low = lax.optimization_barrier((a_matrix / trace_level).astype(jnp.bfloat16))
    inv_root = (inverse_root(start_low) / jnp.sqrt(trace_level)).astype(jnp.bfloat16)
    inner_vec = jnp.dot(inv_root, (drive_vec / divisor).astype(jnp.bfloat16), preferred_element_type=jnp.float32)
    mean_weights = jnp.dot(inv_root, inner_vec.astype(jnp.bfloat16), preferred_element_type=jnp.float32)
    return (inv_root.astype(jnp.float32) + mean_weights[:, None]).astype(jnp.bfloat16)

def solve_patch(selected, innov_rows, weight_rows, tapers, live_count, background):
    live_mask = (jnp.arange(LMAX, dtype=jnp.int32) < live_count).astype(jnp.float32)
    obs_factor = weight_rows.astype(jnp.float32) * (tapers * live_mask)[:, None]
    weighted = (selected * obs_factor.reshape(-1)).astype(jnp.bfloat16)
    gram_mat = lax.dot_general(weighted, selected, (((1,), (1,)), ((), ())), preferred_element_type=jnp.float32)
    drive_vec = jnp.dot(weighted, innov_rows.reshape(-1), preferred_element_type=jnp.float32)
    weights = weights_from_gram(gram_mat, drive_vec)
    return lax.dot_general(weights, background, (((0,), (0,)), ((), ())), preferred_element_type=jnp.float32).astype(jnp.bfloat16)

def reference(ens_obs, innovation, obs_weight, loc_list, counts, taper, state):
    window_span = 3 * BLN

    def one_group(group):
        lon_index = group // N_LAT
        band_index = group % N_LAT
        window_cols = (lon_index * BLN - BLN + jnp.arange(window_span, dtype=jnp.int32)) % NBLON
        row_first = (band_index * BLT).astype(jnp.int32)
        ens_band = lax.dynamic_slice_in_dim(ens_obs, row_first, BLT, 1)
        ens_window = jnp.take(ens_band, window_cols, axis=2).reshape(MEMBERS, BLT * window_span, OBS_BLK)
        innov_window = jnp.take(lax.dynamic_slice_in_dim(innovation, row_first, BLT, 0), window_cols, axis=1).reshape(BLT * window_span, OBS_BLK)
        weight_window = jnp.take(lax.dynamic_slice_in_dim(obs_weight, row_first, BLT, 0), window_cols, axis=1).reshape(BLT * window_span, OBS_BLK)

        def one_patch(patch):
            listed = loc_list[patch, group]
            selected = ens_window[:, listed, :].reshape(MEMBERS, LMAX * OBS_BLK)
            return solve_patch(selected, innov_window[listed], weight_window[listed], taper[patch, group], counts[patch, group], state[:, patch, group, :])
        return lax.map(one_patch, jnp.arange(P_GRP, dtype=jnp.int32))
    results = lax.map(one_group, jnp.arange(GROUPS, dtype=jnp.int32))
    return jnp.transpose(results, (2, 1, 0, 3))
```

```python
import functools

import jax
import jax.numpy as jnp
from jax import lax
from jax.experimental import pallas as pl
from jax.experimental.pallas import tpu as pltpu
from jax.sharding import PartitionSpec as P

MESH = pl.DeviceIdType.MESH
ZN, XN, YN = 8, 4, 4
PEERS = ZN * XN
ROWS = 32
MEMBERS = 1024
OBS = 512
BLK = 128
SLOTS = 4
SDIM = 1280
TILE = 256
SELF_STEP = 4


def kernel(
    obs_ref, side_ref, loc_ref, cnt_ref, tap_ref, state_ref, out_ref,
    win, wside, pick, xfull, wgt, sfull, yroot, zroot, ynext, wmat, omat,
    halo_send, halo_recv, side_send, side_recv,
    ens_send, ens_recv, st_send, st_recv, out_send, out_recv, loc_sem,
):
    me = lax.axis_index("mem")
    zc, xc = me // XN, me % XN
    yc = lax.axis_index("lon")

    def peer(dz, dx):
        return ((zc + dz) % ZN) * XN + (xc + dx) % XN

    def offset(k):
        dz = (4 + 3 * (k % ZN)) % ZN
        return dz, (k // ZN + dz) % XN

    y_up, y_down = (yc + 1) % YN, (yc + YN - 1) % YN

    barrier = pltpu.get_barrier_semaphore()

    def greet(k, carry):
        dz, dx = offset(k)
        pl.semaphore_signal(
            barrier, inc=1, device_id={"mem": peer(dz, dx)}, device_id_type=MESH
        )
        return carry

    lax.fori_loop(0, SELF_STEP, greet, 0)
    lax.fori_loop(SELF_STEP + 1, PEERS, greet, 0)
    for other in (y_up, y_down):
        pl.semaphore_signal(barrier, inc=1, device_id={"lon": other}, device_id_type=MESH)
    pl.semaphore_wait(barrier, PEERS - 1 + 2)

    halo = []
    for slot, other in ((0, y_up), (2, y_down)):
        i = slot // 2
        halo.append(
            pltpu.make_async_remote_copy(
                src_ref=obs_ref, dst_ref=win.at[slot],
                send_sem=halo_send.at[i], recv_sem=halo_recv.at[i],
                device_id={"lon": other}, device_id_type=MESH,
            )
        )
        halo.append(
            pltpu.make_async_remote_copy(
                src_ref=side_ref, dst_ref=wside.at[slot],
                send_sem=side_send.at[i], recv_sem=side_recv.at[i],
                device_id={"lon": other}, device_id_type=MESH,
            )
        )
    for copy in halo:
        copy.start()

    my_rows = pl.ds(pl.multiple_of(me * ROWS, ROWS), ROWS)

    def state_copy(k):
        dz, dx = offset(k)
        to = peer(dz, dx)
        return pltpu.make_async_remote_copy(
            src_ref=state_ref.at[to], dst_ref=sfull.at[my_rows],
            send_sem=st_send.at[k], recv_sem=st_recv.at[k],
            device_id={"mem": to}, device_id_type=MESH,
        )

    def ens_copy(k):
        dz, dx = offset(k)
        to = peer(dz, dx)
        return pltpu.make_async_remote_copy(
            src_ref=pick.at[to], dst_ref=xfull.at[my_rows],
            send_sem=ens_send.at[k], recv_sem=ens_recv.at[k],
            device_id={"mem": to}, device_id_type=MESH,
        )

    def start(make):
        def body(k, carry):
            make(k).start()
            return carry
        return body

    def wait_recv(make):
        def body(k, carry):
            make(k).wait_recv()
            return carry
        return body

    def wait_send(make):
        def body(k, carry):
            make(k).wait_send()
            return carry
        return body

    def others(body):
        lax.fori_loop(0, SELF_STEP, body, 0)
        lax.fori_loop(SELF_STEP + 1, PEERS, body, 0)

    own_state = pltpu.make_async_copy(state_ref.at[me], sfull.at[my_rows], loc_sem.at[0])
    own_state.start()
    lax.fori_loop(0, SELF_STEP, start(state_copy), 0)

    win[1] = obs_ref[...]
    wside[1] = side_ref[...]
    for copy in halo:
        copy.wait()

    def block_index(number):
        row = (number * 43) >> 9
        col = number - row * 12
        group = col >> 2
        return group, row * 4 + (col - group * 4)

    def pick_patch(p, carry):
        for j in range(SLOTS):
            group, block = block_index(loc_ref[p * SLOTS + j])
            pick[p, :, j * BLK : (j + 1) * BLK] = win[group, block]
        return carry

    lax.fori_loop(0, PEERS, pick_patch, 0)
    others(start(ens_copy))
    xfull[my_rows, :] = pick[me]
    lax.fori_loop(SELF_STEP + 1, PEERS, start(state_copy), 0)

    count = cnt_ref[0]
    factors, innovs = [], []
    for j in range(SLOTS):
        group, block = block_index(loc_ref[me * SLOTS + j])
        level = jnp.where(j < count, tap_ref[j], 0.0)
        innovs.append(wside[group, pl.ds(block, 1), :])
        factors.append(wside[group, pl.ds(block + 16, 1), :] * level)
    factor = jnp.concatenate(factors, axis=1)
    innov = jnp.concatenate(innovs, axis=1)

    others(wait_recv(ens_copy))

    drives = []
    total = jnp.zeros((1, 1), jnp.float32)
    for t in range(MEMBERS // TILE):
        rows = pl.ds(t * TILE, TILE)
        selected = xfull[rows, :].astype(jnp.float32)
        weighted = (selected * factor).astype(jnp.bfloat16)
        wgt[rows, :] = weighted
        weighted = weighted.astype(jnp.float32)
        drives.append(jnp.sum(weighted * innov, axis=1, keepdims=True))
        total += jnp.sum(
            jnp.sum(weighted * selected, axis=1, keepdims=True), axis=0, keepdims=True
        )
    divisor = float(MEMBERS - 1)
    level = 2.0 + total * (2.0 / (divisor * MEMBERS))
    inv_level = 1.0 / level
    inv_sqrt = 1.0 / jnp.sqrt(level)

    def eye(t):
        row = lax.broadcasted_iota(jnp.int32, (TILE, MEMBERS), 0) + t * TILE
        col = lax.broadcasted_iota(jnp.int32, (TILE, MEMBERS), 1)
        return jnp.where(row == col, 1.0, 0.0).astype(jnp.float32)

    def tile_rows(t):
        return pl.ds(pl.multiple_of(t * TILE, TILE), TILE)

    def gram_step(t, carry):
        rows = tile_rows(t)
        gram = lax.dot_general(
            wgt[rows, :], xfull[...], (((1,), (1,)), ((), ())),
            preferred_element_type=jnp.float32,
        )
        unit = eye(t)
        low = ((unit + gram * (1.0 / divisor)) * inv_level).astype(jnp.bfloat16)
        yroot[rows, :] = low
        zroot[rows, :] = (0.5 * (3.0 * unit - low.astype(jnp.float32))).astype(jnp.bfloat16)
        return carry

    lax.fori_loop(0, MEMBERS // TILE, gram_step, 0)

    def y_step(t, carry):
        rows = tile_rows(t)
        ynext[rows, :] = jnp.dot(
            yroot[rows, :], zroot[...], preferred_element_type=jnp.float32
        ).astype(jnp.bfloat16)
        return carry

    lax.fori_loop(0, MEMBERS // TILE, y_step, 0)

    def root_step(t, carry):
        rows = tile_rows(t)
        product = jnp.dot(zroot[rows, :], ynext[...], preferred_element_type=jnp.float32)
        half = (0.5 * (3.0 * eye(t) - product)).astype(jnp.bfloat16)
        last = jnp.dot(half, zroot[...], preferred_element_type=jnp.float32)
        yroot[rows, :] = (last * inv_sqrt).astype(jnp.bfloat16)
        return carry

    lax.fori_loop(0, MEMBERS // TILE, root_step, 0)

    drive = jnp.concatenate(drives, axis=0) * (1.0 / divisor)
    drive = jnp.broadcast_to(drive, (MEMBERS, BLK)).astype(jnp.bfloat16)
    inner = jnp.dot(yroot[...], drive, preferred_element_type=jnp.float32)
    mean = jnp.dot(yroot[...], inner.astype(jnp.bfloat16), preferred_element_type=jnp.float32)
    for t in range(MEMBERS // TILE):
        rows = pl.ds(t * TILE, TILE)
        full = yroot[rows, :].astype(jnp.float32) + mean[t * TILE : (t + 1) * TILE, 0:1]
        wmat[:, t * TILE : (t + 1) * TILE] = full.T.astype(jnp.bfloat16)

    others(wait_recv(state_copy))
    own_state.wait()

    def out_copy(k, dz, dx):
        to = peer(dz, dx)
        return pltpu.make_async_remote_copy(
            src_ref=omat.at[pl.ds(pl.multiple_of(to * ROWS, ROWS), ROWS)],
            dst_ref=out_ref.at[me],
            send_sem=out_send.at[k], recv_sem=out_recv.at[k],
            device_id={"mem": to}, device_id_type=MESH,
        )

    plane = XN * ROWS
    sends = []
    for pair in ((4, 3), (5, 2), (6, 1), (7, 0)):
        starts = [pl.multiple_of(((zc + dz) % ZN) * plane, plane) for dz in pair]
        left = jnp.concatenate([wmat[pl.ds(s, plane), :] for s in starts], axis=0)
        block = jnp.dot(left, sfull[...], preferred_element_type=jnp.float32)
        block = block.astype(jnp.bfloat16)
        for i, s in enumerate(starts):
            omat[pl.ds(s, plane), :] = block[i * plane : (i + 1) * plane, :]
        for dx in range(XN):
            for dz in pair:
                if dz or dx:
                    copy = out_copy(dz * XN + dx, dz, dx)
                    copy.start()
                    sends.append(copy)
    own_out = pltpu.make_async_copy(omat.at[my_rows], out_ref.at[me], loc_sem.at[1])
    own_out.start()

    others(wait_send(ens_copy))
    others(wait_send(state_copy))
    for copy in sends:
        copy.wait()
    own_out.wait()


def on_device(ens_obs, innovation, obs_weight, loc_list, counts, taper, state):
    local, rows, cols, blk = ens_obs.shape
    patches = loc_list.shape[0]
    obs = jnp.transpose(ens_obs, (1, 2, 0, 3)).reshape(rows * cols, local, blk)
    side = jnp.concatenate(
        [innovation.reshape(rows * cols, blk), obs_weight.reshape(rows * cols, blk)], axis=0
    ).astype(jnp.float32)
    by_patch = jnp.transpose(state.reshape(local, patches, SDIM), (1, 0, 2))
    vmem = pl.BlockSpec(memory_space=pltpu.VMEM)
    smem = pl.BlockSpec(memory_space=pltpu.SMEM)
    anywhere = pl.BlockSpec(memory_space=pl.ANY)
    dma = pltpu.SemaphoreType.DMA
    low = jnp.bfloat16
    out = pl.pallas_call(
        kernel,
        out_shape=jax.ShapeDtypeStruct((patches, local, SDIM), low),
        in_specs=[vmem, vmem, smem, smem, smem, anywhere],
        out_specs=anywhere,
        scratch_shapes=[
            pltpu.VMEM((3, rows * cols, local, blk), low),
            pltpu.VMEM((3, 2 * rows * cols, blk), jnp.float32),
            pltpu.VMEM((PEERS, local, OBS), low),
            pltpu.VMEM((MEMBERS, OBS), low),
            pltpu.VMEM((MEMBERS, OBS), low),
            pltpu.VMEM((MEMBERS, SDIM), low),
            pltpu.VMEM((MEMBERS, MEMBERS), low),
            pltpu.VMEM((MEMBERS, MEMBERS), low),
            pltpu.VMEM((MEMBERS, MEMBERS), low),
            pltpu.VMEM((MEMBERS, MEMBERS), low),
            pltpu.VMEM((MEMBERS, SDIM), low),
            dma((2,)), dma((2,)), dma((2,)), dma((2,)),
            dma((PEERS,)), dma((PEERS,)), dma((PEERS,)), dma((PEERS,)),
            dma((PEERS,)), dma((PEERS,)), dma((2,)),
        ],
        name="analysis",
        compiler_params=pltpu.CompilerParams(
            collective_id=0, has_side_effects=True, vmem_limit_bytes=56 << 20
        ),
    )(obs, side, loc_list.reshape(-1), counts.reshape(-1), taper.reshape(-1), by_patch)
    return jnp.transpose(out, (1, 0, 2)).reshape(local, patches, 1, SDIM)


def solution(mesh):
    return jax.shard_map(
        on_device,
        mesh=mesh,
        in_specs=(
            P("mem", "lat", "lon", None),
            P("lat", "lon", None),
            P("lat", "lon", None),
            P(None, ("lon", "lat"), None),
            P("mem", ("lon", "lat")),
            P("mem", ("lon", "lat"), None),
            P("mem", None, ("lon", "lat"), None),
        ),
        out_specs=P("mem", None, ("lon", "lat"), None),
        check_vma=False,
    )
```

```python
import functools

import jax
import jax.numpy as jnp
from jax import lax
from jax.experimental import pallas as pl
from jax.experimental.pallas import tpu as pltpu
from jax.sharding import PartitionSpec as P

MESH = pl.DeviceIdType.MESH
ZN, XN, YN = 8, 4, 4
PEERS = ZN * XN
ROWS = 32
MEMBERS = 1024
OBS = 512
BLK = 128
SLOTS = 4
SDIM = 1280
TILE = 256
STARTS = (3, 6, 9, 14)


def kernel(
    ens_ref, innov_ref, wt_ref, loc_ref, cnt_ref, tap_ref, state_ref, out_ref,
    win0, win1, win2, win3, win4, win5, win6, win7, wside, pick, xfull, wgt, snat, spat, sfull, yroot, zroot, ynext, wmat, omat,
    ring_send, ring_recv, y_send, y_recv, side_send, side_recv,
    ens_send, ens_recv, st_send, st_recv, out_send, out_recv, nat_sem, loc_sem,
):
    wins = (win0, win1, win2, win3, win4, win5, win6, win7)
    me = lax.axis_index("mem")
    zc, xc = me // XN, me % XN
    yc = lax.axis_index("lon")
    sign = 1 - 2 * lax.axis_index("lat")

    def peer(dz, dx):
        return ((zc + dz) % ZN) * XN + (xc + dx) % XN

    def offset(k):
        lane = k % (ZN - 1)
        dz = (4 + 3 * (lane + lane // 4)) % ZN
        return dz, (k // (ZN - 1) + dz) % XN

    far = (ZN - 1) * XN
    y_up, y_down = (yc + 1) % YN, (yc + YN - 1) % YN

    group = 8
    natural = []
    for q in range(PEERS // group):
        copy = pltpu.make_async_copy(
            state_ref.at[:, pl.ds(q * group, group), :],
            snat.at[:, pl.ds(q * group, group), :], nat_sem.at[q],
        )
        copy.start()
        natural.append(copy)

    barrier = pltpu.get_barrier_semaphore()

    def greet(k, carry):
        dz, dx = offset(k)
        pl.semaphore_signal(
            barrier, inc=1, device_id={"mem": peer(dz, dx)}, device_id_type=MESH
        )
        return carry

    lax.fori_loop(0, far, greet, 0)
    for dx in range(1, XN):
        pl.semaphore_signal(
            barrier, inc=1, device_id={"mem": peer(0, dx)}, device_id_type=MESH
        )
    for other in (y_up, y_down):
        pl.semaphore_signal(barrier, inc=1, device_id={"lon": other}, device_id_type=MESH)

    wins[4][1] = jnp.swapaxes(ens_ref[...], 0, 1)
    wside[1, 0:16] = innov_ref[...].astype(jnp.float32)
    wside[1, 16:32] = wt_ref[...].astype(jnp.float32)
    pl.semaphore_wait(barrier, PEERS - 1 + 2)

    def unit(r):
        return (zc + sign * r + ZN) % ZN

    def ring_copy(arm, s):
        r = -s if arm == 0 else s
        r_there = r - 1 if arm == 0 else r + 1
        to = ((zc + sign * (1 - 2 * arm) + ZN) % ZN) * XN + xc
        i = arm * 4 + s
        return pltpu.make_async_remote_copy(
            src_ref=wins[r + 4].at[1], dst_ref=wins[r_there + 4].at[1],
            send_sem=ring_send.at[i], recv_sem=ring_recv.at[i],
            device_id={"mem": to}, device_id_type=MESH,
        )

    def y_copies(r):
        i = r + 4
        return [
            pltpu.make_async_remote_copy(
                src_ref=wins[i].at[1], dst_ref=wins[i].at[slot],
                send_sem=y_send.at[slot // 2, i], recv_sem=y_recv.at[slot // 2, i],
                device_id={"lon": other}, device_id_type=MESH,
            )
            for slot, other in ((0, y_up), (2, y_down))
        ]

    sides = [
        pltpu.make_async_remote_copy(
            src_ref=wside.at[1], dst_ref=wside.at[slot],
            send_sem=side_send.at[slot // 2], recv_sem=side_recv.at[slot // 2],
            device_id={"lon": other}, device_id_type=MESH,
        )
        for slot, other in ((0, y_up), (2, y_down))
    ]

    my_rows = pl.ds(pl.multiple_of(me * ROWS, ROWS), ROWS)

    def state_send(sem, dz, dx):
        to = peer(dz, dx)
        return pltpu.make_async_remote_copy(
            src_ref=spat.at[to], dst_ref=sfull.at[my_rows],
            send_sem=st_send.at[sem], recv_sem=st_recv.at[sem],
            device_id={"mem": to}, device_id_type=MESH,
        )

    def state_copy(k):
        return state_send(k, *offset(k))

    def start(make):
        def body(k, carry):
            make(k).start()
            return carry
        return body

    def wait_recv(make):
        def body(k, carry):
            make(k).wait_recv()
            return carry
        return body

    def wait_send(make):
        def body(k, carry):
            make(k).wait_send()
            return carry
        return body

    ring = {(0, 0): ring_copy(0, 0), (1, 0): ring_copy(1, 0)}
    rows_out = {0: y_copies(0)}
    for copy in list(ring.values()) + rows_out[0] + sides:
        copy.start()

    lanes = 128
    for q in range(PEERS // group):
        natural[q].wait()

        def relayout(t, carry):
            cols = pl.ds(pl.multiple_of(t * lanes, lanes), lanes)
            own = snat[:, q * group : (q + 1) * group, cols]
            spat[q * group : (q + 1) * group, :, cols] = jnp.swapaxes(own, 0, 1)
            return carry

        lax.fori_loop(0, SDIM // lanes, relayout, 0)

    own_state = pltpu.make_async_copy(spat.at[me], sfull.at[my_rows], loc_sem.at[0])
    own_state.start()
    near = [state_send(far + dx - 1, 0, dx) for dx in range(1, XN)]
    for copy in near:
        copy.start()

    done = 0
    for s in range(1, 5):
        for arm in (0, 1):
            if arm == 1 and s == 4:
                continue
            r = -s if arm == 0 else s
            ring[arm, s - 1].wait_recv()
            if s < 4 - arm:
                ring[arm, s] = ring_copy(arm, s)
                ring[arm, s].start()
            rows_out[r] = y_copies(r)
            for copy in rows_out[r]:
                copy.start()
        more = STARTS[s - 1]
        lax.fori_loop(done, more, start(state_copy), 0)
        done = more

    def block_index(number):
        row = (number * 43) >> 9
        col = number - row * 12
        third = col >> 2
        return third, row * 4 + (col - third * 4)

    listed = [
        [block_index(loc_ref[j, zc * XN + (xc + dx) % XN]) for j in range(SLOTS)]
        for dx in range(XN)
    ]

    def full_rows(r, x):
        return pl.ds(pl.multiple_of((unit(r) * XN + x) * ROWS, ROWS), ROWS)

    def ens_copy(dx, r):
        i = r + 4
        return pltpu.make_async_remote_copy(
            src_ref=pick.at[dx - 1, i], dst_ref=xfull.at[full_rows(r, xc)],
            send_sem=ens_send.at[dx - 1, i], recv_sem=ens_recv.at[dx - 1, i],
            device_id={"mem": zc * XN + (xc + dx) % XN}, device_id_type=MESH,
        )

    picked = []
    for r in (0, -1, 1, -2, 2, -3, 3, -4):
        for copy in rows_out[r]:
            copy.wait_recv()
        for dx in (1, 2, 3, 0):
            for j in range(SLOTS):
                third, block = listed[dx][j]
                tile = wins[r + 4][third, block]
                cols = slice(j * BLK, (j + 1) * BLK)
                if dx:
                    pick[dx - 1, r + 4, :, cols] = tile
                else:
                    xfull[full_rows(r, xc), cols] = tile
            if dx:
                copy = ens_copy(dx, r)
                copy.start()
                picked.append(copy)
    lax.fori_loop(done, far, start(state_copy), 0)
    for copy in sides:
        copy.wait_recv()

    count = cnt_ref[0]
    factors, innovs = [], []
    for j in range(SLOTS):
        third, block = listed[0][j]
        level = jnp.where(j < count, tap_ref[j], 0.0)
        innovs.append(wside[third, pl.ds(block, 1), :])
        factors.append(wside[third, pl.ds(block + 16, 1), :] * level)
    factor = jnp.concatenate(factors, axis=1)
    innov = jnp.concatenate(innovs, axis=1)

    for copy in picked:
        copy.wait_recv()

    drives = []
    total = jnp.zeros((1, 1), jnp.float32)
    for t in range(MEMBERS // TILE):
        rows = pl.ds(t * TILE, TILE)
        selected = xfull[rows, :].astype(jnp.float32)
        weighted = (selected * factor).astype(jnp.bfloat16)
        wgt[rows, :] = weighted
        weighted = weighted.astype(jnp.float32)
        drives.append(jnp.sum(weighted * innov, axis=1, keepdims=True))
        total += jnp.sum(
            jnp.sum(weighted * selected, axis=1, keepdims=True), axis=0, keepdims=True
        )
    divisor = float(MEMBERS - 1)
    level = 2.0 + total * (2.0 / (divisor * MEMBERS))
    inv_level = 1.0 / level
    inv_sqrt = 1.0 / jnp.sqrt(level)

    def eye(t):
        row = lax.broadcasted_iota(jnp.int32, (TILE, MEMBERS), 0) + t * TILE
        col = lax.broadcasted_iota(jnp.int32, (TILE, MEMBERS), 1)
        return jnp.where(row == col, 1.0, 0.0).astype(jnp.float32)

    def tile_rows(t):
        return pl.ds(pl.multiple_of(t * TILE, TILE), TILE)

    def gram_step(t, carry):
        rows = tile_rows(t)
        gram = lax.dot_general(
            wgt[rows, :], xfull[...], (((1,), (1,)), ((), ())),
            preferred_element_type=jnp.float32,
        )
        unit = eye(t)
        low = ((unit + gram * (1.0 / divisor)) * inv_level).astype(jnp.bfloat16)
        yroot[rows, :] = low
        zroot[rows, :] = (0.5 * (3.0 * unit - low.astype(jnp.float32))).astype(jnp.bfloat16)
        return carry

    lax.fori_loop(0, MEMBERS // TILE, gram_step, 0)

    def y_step(t, carry):
        rows = tile_rows(t)
        ynext[rows, :] = jnp.dot(
            yroot[rows, :], zroot[...], preferred_element_type=jnp.float32
        ).astype(jnp.bfloat16)
        return carry

    lax.fori_loop(0, MEMBERS // TILE, y_step, 0)

    def root_step(t, carry):
        rows = tile_rows(t)
        product = jnp.dot(zroot[rows, :], ynext[...], preferred_element_type=jnp.float32)
        half = (0.5 * (3.0 * eye(t) - product)).astype(jnp.bfloat16)
        last = jnp.dot(half, zroot[...], preferred_element_type=jnp.float32)
        yroot[rows, :] = (last * inv_sqrt).astype(jnp.bfloat16)
        return carry

    lax.fori_loop(0, MEMBERS // TILE, root_step, 0)

    drive = jnp.concatenate(drives, axis=0) * (1.0 / divisor)
    drive = jnp.broadcast_to(drive, (MEMBERS, BLK)).astype(jnp.bfloat16)
    inner = jnp.dot(yroot[...], drive, preferred_element_type=jnp.float32)
    mean = jnp.dot(yroot[...], inner.astype(jnp.bfloat16), preferred_element_type=jnp.float32)
    for t in range(MEMBERS // TILE):
        rows = pl.ds(t * TILE, TILE)
        full = yroot[rows, :].astype(jnp.float32) + mean[t * TILE : (t + 1) * TILE, 0:1]
        wmat[:, t * TILE : (t + 1) * TILE] = full.T.astype(jnp.bfloat16)

    lax.fori_loop(0, far, wait_recv(state_copy), 0)
    for copy in near:
        copy.wait_recv()
    own_state.wait()

    def out_copy(k, dz, dx):
        to = peer(dz, dx)
        return pltpu.make_async_remote_copy(
            src_ref=omat.at[pl.ds(pl.multiple_of(to * ROWS, ROWS), ROWS)],
            dst_ref=out_ref.at[me],
            send_sem=out_send.at[k], recv_sem=out_recv.at[k],
            device_id={"mem": to}, device_id_type=MESH,
        )

    plane = XN * ROWS
    sends = []
    for pair in ((4, 3), (5, 2), (6, 1), (7, 0)):
        starts = [pl.multiple_of(((zc + dz) % ZN) * plane, plane) for dz in pair]
        left = jnp.concatenate([wmat[pl.ds(s, plane), :] for s in starts], axis=0)
        block = jnp.dot(left, sfull[...], preferred_element_type=jnp.float32)
        block = block.astype(jnp.bfloat16)
        for i, s in enumerate(starts):
            omat[pl.ds(s, plane), :] = block[i * plane : (i + 1) * plane, :]
        for dx in range(XN):
            for dz in pair:
                if dz or dx:
                    copy = out_copy(dz * XN + dx, dz, dx)
                    copy.start()
                    sends.append(copy)
    own_out = pltpu.make_async_copy(omat.at[my_rows], out_ref.at[me], loc_sem.at[1])
    own_out.start()

    lax.fori_loop(0, far, wait_send(state_copy), 0)
    early = list(ring.values()) + sides + near + picked
    for copies in rows_out.values():
        early += copies
    for copy in early:
        copy.wait_send()
    for copy in sends:
        copy.wait()
    own_out.wait()


def on_device(ens_obs, innovation, obs_weight, loc_list, counts, taper, state):
    local, rows, cols, blk = ens_obs.shape
    blocks = rows * cols
    patches = loc_list.shape[0]
    vmem = pl.BlockSpec(memory_space=pltpu.VMEM)
    smem = pl.BlockSpec(memory_space=pltpu.SMEM)
    anywhere = pl.BlockSpec(memory_space=pl.ANY)
    dma = pltpu.SemaphoreType.DMA
    low = jnp.bfloat16
    out = pl.pallas_call(
        kernel,
        out_shape=jax.ShapeDtypeStruct((patches, local, SDIM), low),
        in_specs=[
            vmem, vmem, vmem, smem, smem, smem,
            pl.BlockSpec(memory_space=pltpu.MemorySpace.HBM),
        ],
        out_specs=anywhere,
        scratch_shapes=[
            *[pltpu.VMEM((3, blocks, local, blk), low)] * ZN,
            pltpu.VMEM((3, 2 * blocks, blk), jnp.float32),
            pltpu.VMEM((XN - 1, ZN, local, OBS), low),
            pltpu.VMEM((MEMBERS, OBS), low),
            pltpu.VMEM((MEMBERS, OBS), low),
            pltpu.VMEM((local, patches, SDIM), low),
            pltpu.VMEM((patches, local, SDIM), low),
            pltpu.VMEM((MEMBERS, SDIM), low),
            pltpu.VMEM((MEMBERS, MEMBERS), low),
            pltpu.VMEM((MEMBERS, MEMBERS), low),
            pltpu.VMEM((MEMBERS, MEMBERS), low),
            pltpu.VMEM((MEMBERS, MEMBERS), low),
            pltpu.VMEM((MEMBERS, SDIM), low),
            dma((7,)), dma((7,)), dma((2, ZN)), dma((2, ZN)), dma((2,)), dma((2,)),
            dma((XN - 1, ZN)), dma((XN - 1, ZN)), dma((PEERS - 1,)), dma((PEERS - 1,)),
            dma((PEERS,)), dma((PEERS,)), dma((4,)), dma((2,)),
        ],
        name="analysis",
        compiler_params=pltpu.CompilerParams(
            collective_id=0, has_side_effects=True, vmem_limit_bytes=36 << 20
        ),
    )(
        ens_obs.reshape(local, blocks, blk), innovation.reshape(blocks, blk),
        obs_weight.reshape(blocks, blk), jnp.transpose(loc_list, (2, 1, 0)).reshape(SLOTS, patches),
        counts.reshape(-1), taper.reshape(-1), state.reshape(local, patches, SDIM),
    )
    return by_member(out).reshape(local, patches, 1, SDIM)


def by_member(patched):
    patches, local, size = patched.shape
    group = 8

    def swap(x_ref, o_ref):
        o_ref[...] = jnp.swapaxes(x_ref[...], 0, 1)

    return pl.pallas_call(
        swap,
        grid=(patches // group,),
        out_shape=jax.ShapeDtypeStruct((local, patches, size), patched.dtype),
        in_specs=[pl.BlockSpec((group, local, size), lambda q: (q, 0, 0))],
        out_specs=pl.BlockSpec((local, group, size), lambda q: (0, q, 0)),
        name="by_member",
        compiler_params=pltpu.CompilerParams(vmem_limit_bytes=12 << 20),
    )(patched)


def solution(mesh):
    return jax.shard_map(
        on_device,
        mesh=mesh,
        in_specs=(
            P("mem", "lat", "lon", None),
            P("lat", "lon", None),
            P("lat", "lon", None),
            P(None, ("lon", "lat"), None),
            P("mem", ("lon", "lat")),
            P("mem", ("lon", "lat"), None),
            P("mem", None, ("lon", "lat"), None),
        ),
        out_specs=P("mem", None, ("lon", "lat"), None),
        check_vma=False,
    )
```

```python
import functools

import jax
import jax.numpy as jnp
from jax import lax
from jax.experimental import pallas as pl
from jax.experimental.pallas import tpu as pltpu
from jax.sharding import PartitionSpec as P

MESH = pl.DeviceIdType.MESH
ZN, XN, YN = 8, 4, 4
PEERS = ZN * XN
ROWS = 32
MEMBERS = 1024
OBS = 512
BLK = 128
SLOTS = 4
SDIM = 1280
TILE = 256
STARTS = (4, 8, 14, 24)
PARTS = ((0, 768), (768, 512))


def kernel(
    ens_ref, innov_ref, wt_ref, loc_ref, cnt_ref, tap_ref, state_ref, out_ref,
    win0, win1, win2, win3, win4, win5, win6, win7, wside, pick, xfull, wgt, snat, spat, sfull, yroot, zroot, ynext, wmat, omat, obuf,
    ring_send, ring_recv, y_send, y_recv, side_send, side_recv,
    ens_send, ens_recv, st_send, st_recv, out_send, out_recv, nat_sem, loc_sem, fin_sem,
):
    wins = (win0, win1, win2, win3, win4, win5, win6, win7)
    me = lax.axis_index("mem")
    zc, xc = me // XN, me % XN
    yc = lax.axis_index("lon")
    sign = 1 - 2 * lax.axis_index("lat")

    def peer(dz, dx):
        return ((zc + dz) % ZN) * XN + (xc + dx) % XN

    def offset(k):
        lane = k % (ZN - 1)
        dz = (4 + 3 * (lane + lane // 4)) % ZN
        return dz, (k // (ZN - 1) + dz) % XN

    far = (ZN - 1) * XN
    y_up, y_down = (yc + 1) % YN, (yc + YN - 1) % YN

    group = 8
    natural = []
    for q in range(PEERS // group):
        copy = pltpu.make_async_copy(
            state_ref.at[:, pl.ds(q * group, group), :],
            snat.at[:, pl.ds(q * group, group), :], nat_sem.at[q],
        )
        copy.start()
        natural.append(copy)

    barrier = pltpu.get_barrier_semaphore()

    def greet(k, carry):
        dz, dx = offset(k)
        pl.semaphore_signal(
            barrier, inc=1, device_id={"mem": peer(dz, dx)}, device_id_type=MESH
        )
        return carry

    lax.fori_loop(0, far, greet, 0)
    for dx in range(1, XN):
        pl.semaphore_signal(
            barrier, inc=1, device_id={"mem": peer(0, dx)}, device_id_type=MESH
        )
    for other in (y_up, y_down):
        pl.semaphore_signal(barrier, inc=1, device_id={"lon": other}, device_id_type=MESH)

    wins[4][1] = jnp.swapaxes(ens_ref[...], 0, 1)
    wside[1, 0:16] = innov_ref[...].astype(jnp.float32)
    wside[1, 16:32] = wt_ref[...].astype(jnp.float32)
    pl.semaphore_wait(barrier, PEERS - 1 + 2)

    def unit(r):
        return (zc + sign * r + ZN) % ZN

    def ring_copy(arm, s):
        r = -s if arm == 0 else s
        r_there = r - 1 if arm == 0 else r + 1
        to = ((zc + sign * (1 - 2 * arm) + ZN) % ZN) * XN + xc
        i = arm * 4 + s
        return pltpu.make_async_remote_copy(
            src_ref=wins[r + 4].at[1], dst_ref=wins[r_there + 4].at[1],
            send_sem=ring_send.at[i], recv_sem=ring_recv.at[i],
            device_id={"mem": to}, device_id_type=MESH,
        )

    def y_copies(r):
        i = r + 4
        return [
            pltpu.make_async_remote_copy(
                src_ref=wins[i].at[1], dst_ref=wins[i].at[slot],
                send_sem=y_send.at[slot // 2, i], recv_sem=y_recv.at[slot // 2, i],
                device_id={"lon": other}, device_id_type=MESH,
            )
            for slot, other in ((0, y_up), (2, y_down))
        ]

    sides = [
        pltpu.make_async_remote_copy(
            src_ref=wside.at[1], dst_ref=wside.at[slot],
            send_sem=side_send.at[slot // 2], recv_sem=side_recv.at[slot // 2],
            device_id={"lon": other}, device_id_type=MESH,
        )
        for slot, other in ((0, y_up), (2, y_down))
    ]

    my_rows = pl.ds(pl.multiple_of(me * ROWS, ROWS), ROWS)

    def state_send(part, sem, dz, dx):
        to = peer(dz, dx)
        cols = pl.ds(*PARTS[part])
        return pltpu.make_async_remote_copy(
            src_ref=spat.at[to, :, cols], dst_ref=sfull.at[my_rows, cols],
            send_sem=st_send.at[part, sem], recv_sem=st_recv.at[part, sem],
            device_id={"mem": to}, device_id_type=MESH,
        )

    def state_copy(part):
        return lambda k: state_send(part, k, *offset(k))

    def start(make):
        def body(k, carry):
            make(k).start()
            return carry
        return body

    def wait_recv(make):
        def body(k, carry):
            make(k).wait_recv()
            return carry
        return body

    def wait_send(make):
        def body(k, carry):
            make(k).wait_send()
            return carry
        return body

    ring = {(0, 0): ring_copy(0, 0), (1, 0): ring_copy(1, 0)}
    rows_out = {0: y_copies(0)}
    for copy in list(ring.values()) + rows_out[0] + sides:
        copy.start()

    lanes = 128
    for q in range(PEERS // group):
        natural[q].wait()

        def relayout(t, carry):
            cols = pl.ds(pl.multiple_of(t * lanes, lanes), lanes)
            own = snat[:, q * group : (q + 1) * group, cols]
            spat[q * group : (q + 1) * group, :, cols] = jnp.swapaxes(own, 0, 1)
            return carry

        lax.fori_loop(0, SDIM // lanes, relayout, 0)

    own_state = pltpu.make_async_copy(spat.at[me], sfull.at[my_rows], loc_sem.at[0])
    own_state.start()
    near = [[state_send(h, far + dx - 1, 0, dx) for dx in range(1, XN)] for h in (0, 1)]
    for copy in near[0]:
        copy.start()

    done = 0
    for s in range(1, 5):
        for arm in (0, 1):
            if arm == 1 and s == 4:
                continue
            r = -s if arm == 0 else s
            ring[arm, s - 1].wait_recv()
            if s < 4 - arm:
                ring[arm, s] = ring_copy(arm, s)
                ring[arm, s].start()
            rows_out[r] = y_copies(r)
            for copy in rows_out[r]:
                copy.start()
        more = STARTS[s - 1]
        lax.fori_loop(done, more, start(state_copy(0)), 0)
        done = more

    def block_index(number):
        row = (number * 43) >> 9
        col = number - row * 12
        third = col >> 2
        return third, row * 4 + (col - third * 4)

    listed = [
        [block_index(loc_ref[j, zc * XN + (xc + dx) % XN]) for j in range(SLOTS)]
        for dx in range(XN)
    ]

    def full_rows(r, x):
        return pl.ds(pl.multiple_of((unit(r) * XN + x) * ROWS, ROWS), ROWS)

    def ens_copy(dx, r):
        i = r + 4
        return pltpu.make_async_remote_copy(
            src_ref=pick.at[dx - 1, i], dst_ref=xfull.at[full_rows(r, xc)],
            send_sem=ens_send.at[dx - 1, i], recv_sem=ens_recv.at[dx - 1, i],
            device_id={"mem": zc * XN + (xc + dx) % XN}, device_id_type=MESH,
        )

    picked = []
    for r in (0, -1, 1, -2, 2, -3, 3, -4):
        for copy in rows_out[r]:
            copy.wait_recv()
        for dx in (1, 2, 3, 0):
            for j in range(SLOTS):
                third, block = listed[dx][j]
                tile = wins[r + 4][third, block]
                cols = slice(j * BLK, (j + 1) * BLK)
                if dx:
                    pick[dx - 1, r + 4, :, cols] = tile
                else:
                    xfull[full_rows(r, xc), cols] = tile
            if dx:
                copy = ens_copy(dx, r)
                copy.start()
                picked.append(copy)
    lax.fori_loop(done, far, start(state_copy(0)), 0)
    for copy in near[1]:
        copy.start()
    lax.fori_loop(0, far, start(state_copy(1)), 0)
    for copy in sides:
        copy.wait_recv()

    count = cnt_ref[0]
    factors, innovs = [], []
    for j in range(SLOTS):
        third, block = listed[0][j]
        level = jnp.where(j < count, tap_ref[j], 0.0)
        innovs.append(wside[third, pl.ds(block, 1), :])
        factors.append(wside[third, pl.ds(block + 16, 1), :] * level)
    factor = jnp.concatenate(factors, axis=1)
    innov = jnp.concatenate(innovs, axis=1)

    for copy in picked:
        copy.wait_recv()

    drives = []
    total = jnp.zeros((1, 1), jnp.float32)
    for t in range(MEMBERS // TILE):
        rows = pl.ds(t * TILE, TILE)
        selected = xfull[rows, :].astype(jnp.float32)
        weighted = (selected * factor).astype(jnp.bfloat16)
        wgt[rows, :] = weighted
        weighted = weighted.astype(jnp.float32)
        drives.append(jnp.sum(weighted * innov, axis=1, keepdims=True))
        total += jnp.sum(
            jnp.sum(weighted * selected, axis=1, keepdims=True), axis=0, keepdims=True
        )
    divisor = float(MEMBERS - 1)
    level = 2.0 + total * (2.0 / (divisor * MEMBERS))
    inv_level = 1.0 / level
    inv_sqrt = 1.0 / jnp.sqrt(level)

    def eye(t):
        row = lax.broadcasted_iota(jnp.int32, (TILE, MEMBERS), 0) + t * TILE
        col = lax.broadcasted_iota(jnp.int32, (TILE, MEMBERS), 1)
        return jnp.where(row == col, 1.0, 0.0).astype(jnp.float32)

    def tile_rows(t):
        return pl.ds(pl.multiple_of(t * TILE, TILE), TILE)

    def gram_step(t, carry):
        rows = tile_rows(t)
        gram = lax.dot_general(
            wgt[rows, :], xfull[...], (((1,), (1,)), ((), ())),
            preferred_element_type=jnp.float32,
        )
        unit = eye(t)
        low = ((unit + gram * (1.0 / divisor)) * inv_level).astype(jnp.bfloat16)
        yroot[rows, :] = low
        zroot[rows, :] = (0.5 * (3.0 * unit - low.astype(jnp.float32))).astype(jnp.bfloat16)
        return carry

    lax.fori_loop(0, MEMBERS // TILE, gram_step, 0)

    def y_step(t, carry):
        rows = tile_rows(t)
        ynext[rows, :] = jnp.dot(
            yroot[rows, :], zroot[...], preferred_element_type=jnp.float32
        ).astype(jnp.bfloat16)
        return carry

    lax.fori_loop(0, MEMBERS // TILE, y_step, 0)

    def root_step(t, carry):
        rows = tile_rows(t)
        product = jnp.dot(zroot[rows, :], ynext[...], preferred_element_type=jnp.float32)
        half = (0.5 * (3.0 * eye(t) - product)).astype(jnp.bfloat16)
        last = jnp.dot(half, zroot[...], preferred_element_type=jnp.float32)
        yroot[rows, :] = (last * inv_sqrt).astype(jnp.bfloat16)
        return carry

    lax.fori_loop(0, MEMBERS // TILE, root_step, 0)

    drive = jnp.concatenate(drives, axis=0) * (1.0 / divisor)
    drive = jnp.broadcast_to(drive, (MEMBERS, BLK)).astype(jnp.bfloat16)
    inner = jnp.dot(yroot[...], drive, preferred_element_type=jnp.float32)
    mean = jnp.dot(yroot[...], inner.astype(jnp.bfloat16), preferred_element_type=jnp.float32)
    for t in range(MEMBERS // TILE):
        rows = pl.ds(t * TILE, TILE)
        full = yroot[rows, :].astype(jnp.float32) + mean[t * TILE : (t + 1) * TILE, 0:1]
        wmat[:, t * TILE : (t + 1) * TILE] = full.T.astype(jnp.bfloat16)

    def out_copy(part, k, dz, dx):
        to = peer(dz, dx)
        cols = pl.ds(*PARTS[part])
        return pltpu.make_async_remote_copy(
            src_ref=omat.at[pl.ds(pl.multiple_of(to * ROWS, ROWS), ROWS), cols],
            dst_ref=obuf.at[me, :, cols],
            send_sem=out_send.at[part, k], recv_sem=out_recv.at[part, k],
            device_id={"mem": to}, device_id_type=MESH,
        )

    own_state.wait()
    plane = XN * ROWS
    sends = []
    for part in (0, 1):
        cols = pl.ds(*PARTS[part])
        lax.fori_loop(0, far, wait_recv(state_copy(part)), 0)
        for copy in near[part]:
            copy.wait_recv()
        for pair in ((4, 3), (5, 2), (6, 1), (7, 0)):
            starts = [pl.multiple_of(((zc + dz) % ZN) * plane, plane) for dz in pair]
            left = jnp.concatenate([wmat[pl.ds(s, plane), :] for s in starts], axis=0)
            block = jnp.dot(left, sfull[:, cols], preferred_element_type=jnp.float32)
            block = block.astype(jnp.bfloat16)
            for i, s in enumerate(starts):
                omat[pl.ds(s, plane), cols] = block[i * plane : (i + 1) * plane, :]
            for dx in range(XN):
                for dz in pair:
                    if dz or dx:
                        copy = out_copy(part, dz * XN + dx, dz, dx)
                        copy.start()
                        sends.append(copy)
    obuf[me] = omat[my_rows, :]

    stores = []
    per_part = PEERS - 1
    for part in (0, 1):
        first, width = PARTS[part]
        for copy in sends[part * per_part : (part + 1) * per_part]:
            copy.wait_recv()
        for q in range(PEERS // group):
            pats = slice(q * group, (q + 1) * group)

            def restore(t, carry):
                cols = pl.ds(pl.multiple_of(first + t * lanes, lanes), lanes)
                snat[:, pats, cols] = jnp.swapaxes(obuf[pats, :, cols], 0, 1)
                return carry

            lax.fori_loop(0, width // lanes, restore, 0)
            copy = pltpu.make_async_copy(
                snat.at[:, pats, pl.ds(first, width)], out_ref.at[:, pats, pl.ds(first, width)],
                fin_sem.at[part, q],
            )
            copy.start()
            stores.append(copy)

    lax.fori_loop(0, far, wait_send(state_copy(0)), 0)
    lax.fori_loop(0, far, wait_send(state_copy(1)), 0)
    early = list(ring.values()) + sides + near[0] + near[1] + picked
    for copies in rows_out.values():
        early += copies
    for copy in early + sends:
        copy.wait_send()
    for copy in stores:
        copy.wait()


def on_device(ens_obs, innovation, obs_weight, loc_list, counts, taper, state):
    local, rows, cols, blk = ens_obs.shape
    blocks = rows * cols
    patches = loc_list.shape[0]
    vmem = pl.BlockSpec(memory_space=pltpu.VMEM)
    smem = pl.BlockSpec(memory_space=pltpu.SMEM)
    anywhere = pl.BlockSpec(memory_space=pl.ANY)
    dma = pltpu.SemaphoreType.DMA
    low = jnp.bfloat16
    out = pl.pallas_call(
        kernel,
        out_shape=jax.ShapeDtypeStruct((local, patches, SDIM), low),
        in_specs=[
            vmem, vmem, vmem, smem, smem, smem,
            pl.BlockSpec(memory_space=pltpu.MemorySpace.HBM),
        ],
        out_specs=anywhere,
        scratch_shapes=[
            *[pltpu.VMEM((3, blocks, local, blk), low)] * ZN,
            pltpu.VMEM((3, 2 * blocks, blk), jnp.float32),
            pltpu.VMEM((XN - 1, ZN, local, OBS), low),
            pltpu.VMEM((MEMBERS, OBS), low),
            pltpu.VMEM((MEMBERS, OBS), low),
            pltpu.VMEM((local, patches, SDIM), low),
            pltpu.VMEM((patches, local, SDIM), low),
            pltpu.VMEM((MEMBERS, SDIM), low),
            pltpu.VMEM((MEMBERS, MEMBERS), low),
            pltpu.VMEM((MEMBERS, MEMBERS), low),
            pltpu.VMEM((MEMBERS, MEMBERS), low),
            pltpu.VMEM((MEMBERS, MEMBERS), low),
            pltpu.VMEM((MEMBERS, SDIM), low),
            pltpu.VMEM((patches, local, SDIM), low),
            dma((7,)), dma((7,)), dma((2, ZN)), dma((2, ZN)), dma((2,)), dma((2,)),
            dma((XN - 1, ZN)), dma((XN - 1, ZN)), dma((2, PEERS - 1)), dma((2, PEERS - 1)),
            dma((2, PEERS)), dma((2, PEERS)), dma((4,)), dma((2,)), dma((2, 4)),
        ],
        name="analysis",
        compiler_params=pltpu.CompilerParams(
            collective_id=0, has_side_effects=True, vmem_limit_bytes=60 << 20
        ),
    )(
        ens_obs.reshape(local, blocks, blk), innovation.reshape(blocks, blk),
        obs_weight.reshape(blocks, blk), jnp.transpose(loc_list, (2, 1, 0)).reshape(SLOTS, patches),
        counts.reshape(-1), taper.reshape(-1), state.reshape(local, patches, SDIM),
    )
    return out.reshape(local, patches, 1, SDIM)


def solution(mesh):
    return jax.shard_map(
        on_device,
        mesh=mesh,
        in_specs=(
            P("mem", "lat", "lon", None),
            P("lat", "lon", None),
            P("lat", "lon", None),
            P(None, ("lon", "lat"), None),
            P("mem", ("lon", "lat")),
            P("mem", ("lon", "lat"), None),
            P("mem", None, ("lon", "lat"), None),
        ),
        out_specs=P("mem", None, ("lon", "lat"), None),
        check_vma=False,
    )
```

```python
import functools

import jax
import jax.numpy as jnp
from jax import lax
from jax.experimental import pallas as pl
from jax.experimental.pallas import tpu as pltpu
from jax.sharding import PartitionSpec as P

MESH = pl.DeviceIdType.MESH
ZN, XN, YN = 8, 4, 4
PEERS = ZN * XN
ROWS = 32
MEMBERS = 1024
OBS = 512
BLK = 128
SLOTS = 4
SDIM = 1280
TILE = 256
STARTS = (4, 8, 14, 24)
PARTS = ((0, 896), (896, 384))


def kernel(
    ens_ref, innov_ref, wt_ref, loc_ref, cnt_ref, tap_ref, state_ref, out_ref,
    win0, win1, win2, win3, win4, win5, win6, win7, wside, pick, xfull, wgt, snat, spat, sfull, yroot, zroot, ynext, wmat, omat, obuf,
    ring_send, ring_recv, y_send, y_recv, side_send, side_recv,
    ens_send, ens_recv, st_send, st_recv, out_send, out_recv, nat_sem, loc_sem,
):
    wins = (win0, win1, win2, win3, win4, win5, win6, win7)
    me = lax.axis_index("mem")
    zc, xc = me // XN, me % XN
    yc = lax.axis_index("lon")
    sign = 1 - 2 * lax.axis_index("lat")

    def peer(dz, dx):
        return ((zc + dz) % ZN) * XN + (xc + dx) % XN

    def offset(k):
        lane = k % (ZN - 1)
        dz = (4 + 3 * (lane + lane // 4)) % ZN
        return dz, (k // (ZN - 1) + dz) % XN

    far = (ZN - 1) * XN
    y_up, y_down = (yc + 1) % YN, (yc + YN - 1) % YN

    group = 8
    natural = []
    for q in range(PEERS // group):
        copy = pltpu.make_async_copy(
            state_ref.at[:, pl.ds(q * group, group), :],
            snat.at[:, pl.ds(q * group, group), :], nat_sem.at[q],
        )
        copy.start()
        natural.append(copy)

    barrier = pltpu.get_barrier_semaphore()

    def greet(k, carry):
        dz, dx = offset(k)
        pl.semaphore_signal(
            barrier, inc=1, device_id={"mem": peer(dz, dx)}, device_id_type=MESH
        )
        return carry

    lax.fori_loop(0, far, greet, 0)
    for dx in range(1, XN):
        pl.semaphore_signal(
            barrier, inc=1, device_id={"mem": peer(0, dx)}, device_id_type=MESH
        )
    for other in (y_up, y_down):
        pl.semaphore_signal(barrier, inc=1, device_id={"lon": other}, device_id_type=MESH)

    wins[4][1] = jnp.swapaxes(ens_ref[...], 0, 1)
    wside[1, 0:16] = innov_ref[...].astype(jnp.float32)
    wside[1, 16:32] = wt_ref[...].astype(jnp.float32)
    pl.semaphore_wait(barrier, PEERS - 1 + 2)

    def unit(r):
        return (zc + sign * r + ZN) % ZN

    def ring_copy(arm, s):
        r = -s if arm == 0 else s
        r_there = r - 1 if arm == 0 else r + 1
        to = ((zc + sign * (1 - 2 * arm) + ZN) % ZN) * XN + xc
        i = arm * 4 + s
        return pltpu.make_async_remote_copy(
            src_ref=wins[r + 4].at[1], dst_ref=wins[r_there + 4].at[1],
            send_sem=ring_send.at[i], recv_sem=ring_recv.at[i],
            device_id={"mem": to}, device_id_type=MESH,
        )

    def y_copies(r):
        i = r + 4
        return [
            pltpu.make_async_remote_copy(
                src_ref=wins[i].at[1], dst_ref=wins[i].at[slot],
                send_sem=y_send.at[slot // 2, i], recv_sem=y_recv.at[slot // 2, i],
                device_id={"lon": other}, device_id_type=MESH,
            )
            for slot, other in ((0, y_up), (2, y_down))
        ]

    sides = [
        pltpu.make_async_remote_copy(
            src_ref=wside.at[1], dst_ref=wside.at[slot],
            send_sem=side_send.at[slot // 2], recv_sem=side_recv.at[slot // 2],
            device_id={"lon": other}, device_id_type=MESH,
        )
        for slot, other in ((0, y_up), (2, y_down))
    ]

    my_rows = pl.ds(pl.multiple_of(me * ROWS, ROWS), ROWS)

    def state_send(part, sem, dz, dx):
        to = peer(dz, dx)
        cols = pl.ds(*PARTS[part])
        return pltpu.make_async_remote_copy(
            src_ref=spat.at[to, :, cols], dst_ref=sfull.at[my_rows, cols],
            send_sem=st_send.at[part, sem], recv_sem=st_recv.at[part, sem],
            device_id={"mem": to}, device_id_type=MESH,
        )

    def state_copy(part):
        return lambda k: state_send(part, k, *offset(k))

    def start(make):
        def body(k, carry):
            make(k).start()
            return carry
        return body

    def wait_recv(make):
        def body(k, carry):
            make(k).wait_recv()
            return carry
        return body

    def wait_send(make):
        def body(k, carry):
            make(k).wait_send()
            return carry
        return body

    ring = {(0, 0): ring_copy(0, 0), (1, 0): ring_copy(1, 0)}
    rows_out = {0: y_copies(0)}
    for copy in list(ring.values()) + rows_out[0] + sides:
        copy.start()

    lanes = 128
    for q in range(PEERS // group):
        natural[q].wait()

        def relayout(t, carry):
            cols = pl.ds(pl.multiple_of(t * lanes, lanes), lanes)
            own = snat[:, q * group : (q + 1) * group, cols]
            spat[q * group : (q + 1) * group, :, cols] = jnp.swapaxes(own, 0, 1)
            return carry

        lax.fori_loop(0, SDIM // lanes, relayout, 0)

    own_state = pltpu.make_async_copy(spat.at[me], sfull.at[my_rows], loc_sem.at[0])
    own_state.start()
    near = [[state_send(h, far + dx - 1, 0, dx) for dx in range(1, XN)] for h in (0, 1)]
    for copy in near[0]:
        copy.start()

    done = 0
    for s in range(1, 5):
        for arm in (0, 1):
            if arm == 1 and s == 4:
                continue
            r = -s if arm == 0 else s
            ring[arm, s - 1].wait_recv()
            if s < 4 - arm:
                ring[arm, s] = ring_copy(arm, s)
                ring[arm, s].start()
            rows_out[r] = y_copies(r)
            for copy in rows_out[r]:
                copy.start()
        more = STARTS[s - 1]
        lax.fori_loop(done, more, start(state_copy(0)), 0)
        done = more

    def block_index(number):
        row = (number * 43) >> 9
        col = number - row * 12
        third = col >> 2
        return third, row * 4 + (col - third * 4)

    listed = [
        [block_index(loc_ref[j, zc * XN + (xc + dx) % XN]) for j in range(SLOTS)]
        for dx in range(XN)
    ]

    def full_rows(r, x):
        return pl.ds(pl.multiple_of((unit(r) * XN + x) * ROWS, ROWS), ROWS)

    def ens_copy(dx, r):
        i = r + 4
        return pltpu.make_async_remote_copy(
            src_ref=pick.at[dx - 1, i], dst_ref=xfull.at[full_rows(r, xc)],
            send_sem=ens_send.at[dx - 1, i], recv_sem=ens_recv.at[dx - 1, i],
            device_id={"mem": zc * XN + (xc + dx) % XN}, device_id_type=MESH,
        )

    picked = []
    for r in (0, -1, 1, -2, 2, -3, 3, -4):
        for copy in rows_out[r]:
            copy.wait_recv()
        for dx in (1, 2, 3, 0):
            for j in range(SLOTS):
                third, block = listed[dx][j]
                tile = wins[r + 4][third, block]
                cols = slice(j * BLK, (j + 1) * BLK)
                if dx:
                    pick[dx - 1, r + 4, :, cols] = tile
                else:
                    xfull[full_rows(r, xc), cols] = tile
            if dx:
                copy = ens_copy(dx, r)
                copy.start()
                picked.append(copy)
    lax.fori_loop(done, far, start(state_copy(0)), 0)
    for copy in near[1]:
        copy.start()
    lax.fori_loop(0, far, start(state_copy(1)), 0)
    for copy in sides:
        copy.wait_recv()

    count = cnt_ref[0]
    factors, innovs = [], []
    for j in range(SLOTS):
        third, block = listed[0][j]
        level = jnp.where(j < count, tap_ref[j], 0.0)
        innovs.append(wside[third, pl.ds(block, 1), :])
        factors.append(wside[third, pl.ds(block + 16, 1), :] * level)
    factor = jnp.concatenate(factors, axis=1)
    innov = jnp.concatenate(innovs, axis=1)

    for copy in picked:
        copy.wait_recv()

    drives = []
    total = jnp.zeros((1, 1), jnp.float32)
    for t in range(MEMBERS // TILE):
        rows = pl.ds(t * TILE, TILE)
        selected = xfull[rows, :].astype(jnp.float32)
        weighted = (selected * factor).astype(jnp.bfloat16)
        wgt[rows, :] = weighted
        weighted = weighted.astype(jnp.float32)
        drives.append(jnp.sum(weighted * innov, axis=1, keepdims=True))
        total += jnp.sum(
            jnp.sum(weighted * selected, axis=1, keepdims=True), axis=0, keepdims=True
        )
    divisor = float(MEMBERS - 1)
    level = 2.0 + total * (2.0 / (divisor * MEMBERS))
    inv_level = 1.0 / level
    inv_sqrt = 1.0 / jnp.sqrt(level)

    def eye(t):
        row = lax.broadcasted_iota(jnp.int32, (TILE, MEMBERS), 0) + t * TILE
        col = lax.broadcasted_iota(jnp.int32, (TILE, MEMBERS), 1)
        return jnp.where(row == col, 1.0, 0.0).astype(jnp.float32)

    def tile_rows(t):
        return pl.ds(pl.multiple_of(t * TILE, TILE), TILE)

    def gram_step(t, carry):
        rows = tile_rows(t)
        gram = lax.dot_general(
            wgt[rows, :], xfull[...], (((1,), (1,)), ((), ())),
            preferred_element_type=jnp.float32,
        )
        unit = eye(t)
        low = ((unit + gram * (1.0 / divisor)) * inv_level).astype(jnp.bfloat16)
        yroot[rows, :] = low
        zroot[rows, :] = (0.5 * (3.0 * unit - low.astype(jnp.float32))).astype(jnp.bfloat16)
        return carry

    lax.fori_loop(0, MEMBERS // TILE, gram_step, 0)

    def y_step(t, carry):
        rows = tile_rows(t)
        ynext[rows, :] = jnp.dot(
            yroot[rows, :], zroot[...], preferred_element_type=jnp.float32
        ).astype(jnp.bfloat16)
        return carry

    lax.fori_loop(0, MEMBERS // TILE, y_step, 0)

    def root_step(t, carry):
        rows = tile_rows(t)
        product = jnp.dot(zroot[rows, :], ynext[...], preferred_element_type=jnp.float32)
        half = (0.5 * (3.0 * eye(t) - product)).astype(jnp.bfloat16)
        last = jnp.dot(half, zroot[...], preferred_element_type=jnp.float32)
        yroot[rows, :] = (last * inv_sqrt).astype(jnp.bfloat16)
        return carry

    lax.fori_loop(0, MEMBERS // TILE, root_step, 0)

    drive = jnp.concatenate(drives, axis=0) * (1.0 / divisor)
    drive = jnp.broadcast_to(drive, (MEMBERS, BLK)).astype(jnp.bfloat16)
    inner = jnp.dot(yroot[...], drive, preferred_element_type=jnp.float32)
    mean = jnp.dot(yroot[...], inner.astype(jnp.bfloat16), preferred_element_type=jnp.float32)
    for t in range(MEMBERS // TILE):
        rows = pl.ds(t * TILE, TILE)
        full = yroot[rows, :].astype(jnp.float32) + mean[t * TILE : (t + 1) * TILE, 0:1]
        wmat[:, t * TILE : (t + 1) * TILE] = full.T.astype(jnp.bfloat16)

    def out_copy(part, k, dz, dx):
        to = peer(dz, dx)
        cols = pl.ds(*PARTS[part])
        return pltpu.make_async_remote_copy(
            src_ref=omat.at[pl.ds(pl.multiple_of(to * ROWS, ROWS), ROWS), cols],
            dst_ref=obuf.at[me, :, cols],
            send_sem=out_send.at[part, k], recv_sem=out_recv.at[part, k],
            device_id={"mem": to}, device_id_type=MESH,
        )

    own_state.wait()
    plane = XN * ROWS
    sends = []
    for part in (0, 1):
        cols = pl.ds(*PARTS[part])
        lax.fori_loop(0, far, wait_recv(state_copy(part)), 0)
        for copy in near[part]:
            copy.wait_recv()
        for pair in ((4, 3), (5, 2), (6, 1), (7, 0)):
            starts = [pl.multiple_of(((zc + dz) % ZN) * plane, plane) for dz in pair]
            left = jnp.concatenate([wmat[pl.ds(s, plane), :] for s in starts], axis=0)
            block = jnp.dot(left, sfull[:, cols], preferred_element_type=jnp.float32)
            block = block.astype(jnp.bfloat16)
            for i, s in enumerate(starts):
                omat[pl.ds(s, plane), cols] = block[i * plane : (i + 1) * plane, :]
            for dx in range(XN):
                for dz in pair:
                    if dz or dx:
                        copy = out_copy(part, dz * XN + dx, dz, dx)
                        copy.start()
                        sends.append(copy)
    obuf[me] = omat[my_rows, :]

    per_part = PEERS - 1
    for part in (0, 1):
        first, width = PARTS[part]
        for copy in sends[part * per_part : (part + 1) * per_part]:
            copy.wait_recv()
        for q in range(PEERS // group):
            pats = slice(q * group, (q + 1) * group)

            def restore(t, carry):
                cols = pl.ds(pl.multiple_of(first + t * lanes, lanes), lanes)
                out_ref[:, pats, cols] = jnp.swapaxes(obuf[pats, :, cols], 0, 1)
                return carry

            lax.fori_loop(0, width // lanes, restore, 0)

    lax.fori_loop(0, far, wait_send(state_copy(0)), 0)
    lax.fori_loop(0, far, wait_send(state_copy(1)), 0)
    early = list(ring.values()) + sides + near[0] + near[1] + picked
    for copies in rows_out.values():
        early += copies
    for copy in early + sends:
        copy.wait_send()


def on_device(ens_obs, innovation, obs_weight, loc_list, counts, taper, state):
    local, rows, cols, blk = ens_obs.shape
    blocks = rows * cols
    patches = loc_list.shape[0]
    vmem = pl.BlockSpec(memory_space=pltpu.VMEM)
    smem = pl.BlockSpec(memory_space=pltpu.SMEM)
    anywhere = pl.BlockSpec(memory_space=pl.ANY)
    dma = pltpu.SemaphoreType.DMA
    low = jnp.bfloat16
    out = pl.pallas_call(
        kernel,
        out_shape=pltpu.VMEM((local, patches, SDIM), low),
        in_specs=[
            vmem, vmem, vmem, smem, smem, smem,
            pl.BlockSpec(memory_space=pltpu.MemorySpace.HBM),
        ],
        out_specs=vmem,
        scratch_shapes=[
            *[pltpu.VMEM((3, blocks, local, blk), low)] * ZN,
            pltpu.VMEM((3, 2 * blocks, blk), jnp.float32),
            pltpu.VMEM((XN - 1, ZN, local, OBS), low),
            pltpu.VMEM((MEMBERS, OBS), low),
            pltpu.VMEM((MEMBERS, OBS), low),
            pltpu.VMEM((local, patches, SDIM), low),
            pltpu.VMEM((patches, local, SDIM), low),
            pltpu.VMEM((MEMBERS, SDIM), low),
            pltpu.VMEM((MEMBERS, MEMBERS), low),
            pltpu.VMEM((MEMBERS, MEMBERS), low),
            pltpu.VMEM((MEMBERS, MEMBERS), low),
            pltpu.VMEM((MEMBERS, MEMBERS), low),
            pltpu.VMEM((MEMBERS, SDIM), low),
            pltpu.VMEM((patches, local, SDIM), low),
            dma((7,)), dma((7,)), dma((2, ZN)), dma((2, ZN)), dma((2,)), dma((2,)),
            dma((XN - 1, ZN)), dma((XN - 1, ZN)), dma((2, PEERS - 1)), dma((2, PEERS - 1)),
            dma((2, PEERS)), dma((2, PEERS)), dma((4,)), dma((2,)),
        ],
        name="analysis",
        compiler_params=pltpu.CompilerParams(
            collective_id=0, has_side_effects=True, vmem_limit_bytes=56 << 20
        ),
    )(
        ens_obs.reshape(local, blocks, blk), innovation.reshape(blocks, blk),
        obs_weight.reshape(blocks, blk), jnp.transpose(loc_list, (2, 1, 0)).reshape(SLOTS, patches),
        counts.reshape(-1), taper.reshape(-1), state.reshape(local, patches, SDIM),
    )
    return out.reshape(local, patches, 1, SDIM)


def solution(mesh):
    return jax.shard_map(
        on_device,
        mesh=mesh,
        in_specs=(
            P("mem", "lat", "lon", None),
            P("lat", "lon", None),
            P("lat", "lon", None),
            P(None, ("lon", "lat"), None),
            P("mem", ("lon", "lat")),
            P("mem", ("lon", "lat"), None),
            P("mem", None, ("lon", "lat"), None),
        ),
        out_specs=P("mem", None, ("lon", "lat"), None),
        check_vma=False,
    )
```

```python
import functools

import jax
import jax.numpy as jnp
from jax import lax
from jax.experimental import pallas as pl
from jax.experimental.pallas import tpu as pltpu
from jax.sharding import PartitionSpec as P

MESH = pl.DeviceIdType.MESH
ZN, XN, YN = 8, 4, 4
PEERS = ZN * XN
ROWS = 32
MEMBERS = 1024
OBS = 512
BLK = 128
SLOTS = 4
SDIM = 1280
TILE = 256
STARTS = (4, 8, 14, 24)
PARTS = ((0, 896), (896, 384))


def kernel(
    ens_ref, innov_ref, wt_ref, loc_ref, cnt_ref, tap_ref, state_ref, out_ref,
    win0, win1, win2, win3, win4, win5, win6, win7, wside, pick, xfull, wgt, snat, spat, sfull, yroot, zroot, ynext, wmat, omat, obuf,
    ring_send, ring_recv, y_send, y_recv, side_send, side_recv,
    ens_send, ens_recv, st_send, st_recv, out_send, out_recv, nat_sem, loc_sem,
):
    wins = (win0, win1, win2, win3, win4, win5, win6, win7)
    me = lax.axis_index("mem")
    zc, xc = me // XN, me % XN
    yc = lax.axis_index("lon")
    sign = 1 - 2 * lax.axis_index("lat")

    def peer(dz, dx):
        return ((zc + dz) % ZN) * XN + (xc + dx) % XN

    def offset(k):
        lane = k % (ZN - 1)
        dz = (4 + 3 * (lane + lane // 4)) % ZN
        return dz, (k // (ZN - 1) + dz) % XN

    far = (ZN - 1) * XN
    y_up, y_down = (yc + 1) % YN, (yc + YN - 1) % YN

    group = 8
    natural = []
    for q in range(PEERS // group):
        copy = pltpu.make_async_copy(
            state_ref.at[:, pl.ds(q * group, group), :],
            snat.at[:, pl.ds(q * group, group), :], nat_sem.at[q],
        )
        copy.start()
        natural.append(copy)

    barrier = pltpu.get_barrier_semaphore()

    def greet(k, carry):
        dz, dx = offset(k)
        pl.semaphore_signal(
            barrier, inc=1, device_id={"mem": peer(dz, dx)}, device_id_type=MESH
        )
        return carry

    lax.fori_loop(0, far, greet, 0)
    for dx in range(1, XN):
        pl.semaphore_signal(
            barrier, inc=1, device_id={"mem": peer(0, dx)}, device_id_type=MESH
        )
    for other in (y_up, y_down):
        pl.semaphore_signal(barrier, inc=1, device_id={"lon": other}, device_id_type=MESH)

    wins[4][1] = jnp.swapaxes(ens_ref[...], 0, 1)
    wside[1, 0:16] = innov_ref[...].astype(jnp.float32)
    wside[1, 16:32] = wt_ref[...].astype(jnp.float32)
    lanes = 128
    for q in range(PEERS // group):
        natural[q].wait()

        def relayout(t, carry):
            cols = pl.ds(pl.multiple_of(t * lanes, lanes), lanes)
            own = snat[:, q * group : (q + 1) * group, cols]
            spat[q * group : (q + 1) * group, :, cols] = jnp.swapaxes(own, 0, 1)
            return carry

        lax.fori_loop(0, SDIM // lanes, relayout, 0)

    pl.semaphore_wait(barrier, PEERS - 1 + 2)

    def unit(r):
        return (zc + sign * r + ZN) % ZN

    def ring_copy(arm, s):
        r = -s if arm == 0 else s
        r_there = r - 1 if arm == 0 else r + 1
        to = ((zc + sign * (1 - 2 * arm) + ZN) % ZN) * XN + xc
        i = arm * 4 + s
        return pltpu.make_async_remote_copy(
            src_ref=wins[r + 4].at[1], dst_ref=wins[r_there + 4].at[1],
            send_sem=ring_send.at[i], recv_sem=ring_recv.at[i],
            device_id={"mem": to}, device_id_type=MESH,
        )

    def y_copies(r):
        i = r + 4
        return [
            pltpu.make_async_remote_copy(
                src_ref=wins[i].at[1], dst_ref=wins[i].at[slot],
                send_sem=y_send.at[slot // 2, i], recv_sem=y_recv.at[slot // 2, i],
                device_id={"lon": other}, device_id_type=MESH,
            )
            for slot, other in ((0, y_up), (2, y_down))
        ]

    sides = [
        pltpu.make_async_remote_copy(
            src_ref=wside.at[1], dst_ref=wside.at[slot],
            send_sem=side_send.at[slot // 2], recv_sem=side_recv.at[slot // 2],
            device_id={"lon": other}, device_id_type=MESH,
        )
        for slot, other in ((0, y_up), (2, y_down))
    ]

    my_rows = pl.ds(pl.multiple_of(me * ROWS, ROWS), ROWS)

    def state_send(part, sem, dz, dx):
        to = peer(dz, dx)
        cols = pl.ds(*PARTS[part])
        return pltpu.make_async_remote_copy(
            src_ref=spat.at[to, :, cols], dst_ref=sfull.at[my_rows, cols],
            send_sem=st_send.at[part, sem], recv_sem=st_recv.at[part, sem],
            device_id={"mem": to}, device_id_type=MESH,
        )

    def state_copy(part):
        return lambda k: state_send(part, k, *offset(k))

    def start(make):
        def body(k, carry):
            make(k).start()
            return carry
        return body

    def wait_recv(make):
        def body(k, carry):
            make(k).wait_recv()
            return carry
        return body

    def wait_send(make):
        def body(k, carry):
            make(k).wait_send()
            return carry
        return body

    ring = {(0, 0): ring_copy(0, 0), (1, 0): ring_copy(1, 0)}
    rows_out = {0: y_copies(0)}
    for copy in list(ring.values()) + rows_out[0] + sides:
        copy.start()

    own_state = pltpu.make_async_copy(spat.at[me], sfull.at[my_rows], loc_sem.at[0])
    own_state.start()
    near = [[state_send(h, far + dx - 1, 0, dx) for dx in range(1, XN)] for h in (0, 1)]
    for copy in near[0]:
        copy.start()

    done = 0
    for s in range(1, 5):
        for arm in (0, 1):
            if arm == 1 and s == 4:
                continue
            r = -s if arm == 0 else s
            ring[arm, s - 1].wait_recv()
            if s < 4 - arm:
                ring[arm, s] = ring_copy(arm, s)
                ring[arm, s].start()
            rows_out[r] = y_copies(r)
            for copy in rows_out[r]:
                copy.start()
        more = STARTS[s - 1]
        lax.fori_loop(done, more, start(state_copy(0)), 0)
        done = more

    def block_index(number):
        row = (number * 43) >> 9
        col = number - row * 12
        third = col >> 2
        return third, row * 4 + (col - third * 4)

    listed = [
        [block_index(loc_ref[j, zc * XN + (xc + dx) % XN]) for j in range(SLOTS)]
        for dx in range(XN)
    ]

    def full_rows(r, x):
        return pl.ds(pl.multiple_of((unit(r) * XN + x) * ROWS, ROWS), ROWS)

    def ens_copy(dx, r):
        i = r + 4
        return pltpu.make_async_remote_copy(
            src_ref=pick.at[dx - 1, i], dst_ref=xfull.at[full_rows(r, xc)],
            send_sem=ens_send.at[dx - 1, i], recv_sem=ens_recv.at[dx - 1, i],
            device_id={"mem": zc * XN + (xc + dx) % XN}, device_id_type=MESH,
        )

    picked = []
    for r in (0, -1, 1, -2, 2, -3, 3, -4):
        for copy in rows_out[r]:
            copy.wait_recv()
        for dx in (1, 2, 3, 0):
            for j in range(SLOTS):
                third, block = listed[dx][j]
                tile = wins[r + 4][third, block]
                cols = slice(j * BLK, (j + 1) * BLK)
                if dx:
                    pick[dx - 1, r + 4, :, cols] = tile
                else:
                    xfull[full_rows(r, xc), cols] = tile
            if dx:
                copy = ens_copy(dx, r)
                copy.start()
                picked.append(copy)
    lax.fori_loop(done, far, start(state_copy(0)), 0)
    for copy in near[1]:
        copy.start()
    lax.fori_loop(0, far, start(state_copy(1)), 0)
    for copy in sides:
        copy.wait_recv()

    count = cnt_ref[0]
    factors, innovs = [], []
    for j in range(SLOTS):
        third, block = listed[0][j]
        level = jnp.where(j < count, tap_ref[j], 0.0)
        innovs.append(wside[third, pl.ds(block, 1), :])
        factors.append(wside[third, pl.ds(block + 16, 1), :] * level)
    factor = jnp.concatenate(factors, axis=1)
    innov = jnp.concatenate(innovs, axis=1)

    for copy in picked:
        copy.wait_recv()

    drives = []
    total = jnp.zeros((1, 1), jnp.float32)
    for t in range(MEMBERS // TILE):
        rows = pl.ds(t * TILE, TILE)
        selected = xfull[rows, :].astype(jnp.float32)
        weighted = (selected * factor).astype(jnp.bfloat16)
        wgt[rows, :] = weighted
        weighted = weighted.astype(jnp.float32)
        drives.append(jnp.sum(weighted * innov, axis=1, keepdims=True))
        total += jnp.sum(
            jnp.sum(weighted * selected, axis=1, keepdims=True), axis=0, keepdims=True
        )
    divisor = float(MEMBERS - 1)
    level = 2.0 + total * (2.0 / (divisor * MEMBERS))
    inv_level = 1.0 / level
    inv_sqrt = 1.0 / jnp.sqrt(level)

    def eye(t):
        row = lax.broadcasted_iota(jnp.int32, (TILE, MEMBERS), 0) + t * TILE
        col = lax.broadcasted_iota(jnp.int32, (TILE, MEMBERS), 1)
        return jnp.where(row == col, 1.0, 0.0).astype(jnp.float32)

    def tile_rows(t):
        return pl.ds(pl.multiple_of(t * TILE, TILE), TILE)

    def gram_step(t, carry):
        rows = tile_rows(t)
        gram = lax.dot_general(
            wgt[rows, :], xfull[...], (((1,), (1,)), ((), ())),
            preferred_element_type=jnp.float32,
        )
        unit = eye(t)
        low = ((unit + gram * (1.0 / divisor)) * inv_level).astype(jnp.bfloat16)
        yroot[rows, :] = low
        zroot[rows, :] = (0.5 * (3.0 * unit - low.astype(jnp.float32))).astype(jnp.bfloat16)
        return carry

    lax.fori_loop(0, MEMBERS // TILE, gram_step, 0)

    def y_step(t, carry):
        rows = tile_rows(t)
        ynext[rows, :] = jnp.dot(
            yroot[rows, :], zroot[...], preferred_element_type=jnp.float32
        ).astype(jnp.bfloat16)
        return carry

    lax.fori_loop(0, MEMBERS // TILE, y_step, 0)

    def root_step(t, carry):
        rows = tile_rows(t)
        product = jnp.dot(zroot[rows, :], ynext[...], preferred_element_type=jnp.float32)
        half = (0.5 * (3.0 * eye(t) - product)).astype(jnp.bfloat16)
        last = jnp.dot(half, zroot[...], preferred_element_type=jnp.float32)
        yroot[rows, :] = (last * inv_sqrt).astype(jnp.bfloat16)
        return carry

    lax.fori_loop(0, MEMBERS // TILE, root_step, 0)

    drive = jnp.concatenate(drives, axis=0) * (1.0 / divisor)
    drive = jnp.broadcast_to(drive, (MEMBERS, BLK)).astype(jnp.bfloat16)
    inner = jnp.dot(yroot[...], drive, preferred_element_type=jnp.float32)
    mean = jnp.dot(yroot[...], inner.astype(jnp.bfloat16), preferred_element_type=jnp.float32)
    for t in range(MEMBERS // TILE):
        rows = pl.ds(t * TILE, TILE)
        full = yroot[rows, :].astype(jnp.float32) + mean[t * TILE : (t + 1) * TILE, 0:1]
        wmat[:, t * TILE : (t + 1) * TILE] = full.T.astype(jnp.bfloat16)

    def out_copy(part, k, dz, dx):
        to = peer(dz, dx)
        cols = pl.ds(*PARTS[part])
        return pltpu.make_async_remote_copy(
            src_ref=omat.at[pl.ds(pl.multiple_of(to * ROWS, ROWS), ROWS), cols],
            dst_ref=obuf.at[me, :, cols],
            send_sem=out_send.at[part, k], recv_sem=out_recv.at[part, k],
            device_id={"mem": to}, device_id_type=MESH,
        )

    own_state.wait()
    plane = XN * ROWS
    sends = []
    for part in (0, 1):
        cols = pl.ds(*PARTS[part])
        lax.fori_loop(0, far, wait_recv(state_copy(part)), 0)
        for copy in near[part]:
            copy.wait_recv()
        for pair in ((4, 3), (5, 2), (6, 1), (7, 0)):
            starts = [pl.multiple_of(((zc + dz) % ZN) * plane, plane) for dz in pair]
            left = jnp.concatenate([wmat[pl.ds(s, plane), :] for s in starts], axis=0)
            block = jnp.dot(left, sfull[:, cols], preferred_element_type=jnp.float32)
            block = block.astype(jnp.bfloat16)
            for i, s in enumerate(starts):
                omat[pl.ds(s, plane), cols] = block[i * plane : (i + 1) * plane, :]
            for dx in range(XN):
                for dz in pair:
                    if dz or dx:
                        copy = out_copy(part, dz * XN + dx, dz, dx)
                        copy.start()
                        sends.append(copy)
    obuf[me] = omat[my_rows, :]

    per_part = PEERS - 1
    for part in (0, 1):
        first, width = PARTS[part]
        for copy in sends[part * per_part : (part + 1) * per_part]:
            copy.wait_recv()
        for q in range(PEERS // group):
            pats = slice(q * group, (q + 1) * group)

            def restore(t, carry):
                cols = pl.ds(pl.multiple_of(first + t * lanes, lanes), lanes)
                out_ref[:, pats, cols] = jnp.swapaxes(obuf[pats, :, cols], 0, 1)
                return carry

            lax.fori_loop(0, width // lanes, restore, 0)

    lax.fori_loop(0, far, wait_send(state_copy(0)), 0)
    lax.fori_loop(0, far, wait_send(state_copy(1)), 0)
    early = list(ring.values()) + sides + near[0] + near[1] + picked
    for copies in rows_out.values():
        early += copies
    for copy in early + sends:
        copy.wait_send()


def on_device(ens_obs, innovation, obs_weight, loc_list, counts, taper, state):
    local, rows, cols, blk = ens_obs.shape
    blocks = rows * cols
    patches = loc_list.shape[0]
    vmem = pl.BlockSpec(memory_space=pltpu.VMEM)
    smem = pl.BlockSpec(memory_space=pltpu.SMEM)
    anywhere = pl.BlockSpec(memory_space=pl.ANY)
    dma = pltpu.SemaphoreType.DMA
    low = jnp.bfloat16
    out = pl.pallas_call(
        kernel,
        out_shape=pltpu.VMEM((local, patches, SDIM), low),
        in_specs=[
            vmem, vmem, vmem, smem, smem, smem,
            pl.BlockSpec(memory_space=pltpu.MemorySpace.HBM),
        ],
        out_specs=vmem,
        scratch_shapes=[
            *[pltpu.VMEM((3, blocks, local, blk), low)] * ZN,
            pltpu.VMEM((3, 2 * blocks, blk), jnp.float32),
            pltpu.VMEM((XN - 1, ZN, local, OBS), low),
            pltpu.VMEM((MEMBERS, OBS), low),
            pltpu.VMEM((MEMBERS, OBS), low),
            pltpu.VMEM((local, patches, SDIM), low),
            pltpu.VMEM((patches, local, SDIM), low),
            pltpu.VMEM((MEMBERS, SDIM), low),
            pltpu.VMEM((MEMBERS, MEMBERS), low),
            pltpu.VMEM((MEMBERS, MEMBERS), low),
            pltpu.VMEM((MEMBERS, MEMBERS), low),
            pltpu.VMEM((MEMBERS, MEMBERS), low),
            pltpu.VMEM((MEMBERS, SDIM), low),
            pltpu.VMEM((patches, local, SDIM), low),
            dma((7,)), dma((7,)), dma((2, ZN)), dma((2, ZN)), dma((2,)), dma((2,)),
            dma((XN - 1, ZN)), dma((XN - 1, ZN)), dma((2, PEERS - 1)), dma((2, PEERS - 1)),
            dma((2, PEERS)), dma((2, PEERS)), dma((4,)), dma((2,)),
        ],
        name="analysis",
        compiler_params=pltpu.CompilerParams(
            collective_id=0, has_side_effects=True, vmem_limit_bytes=56 << 20
        ),
    )(
        ens_obs.reshape(local, blocks, blk), innovation.reshape(blocks, blk),
        obs_weight.reshape(blocks, blk), jnp.transpose(loc_list, (2, 1, 0)).reshape(SLOTS, patches),
        counts.reshape(-1), taper.reshape(-1), state.reshape(local, patches, SDIM),
    )
    return out.reshape(local, patches, 1, SDIM)


def solution(mesh):
    return jax.shard_map(
        on_device,
        mesh=mesh,
        in_specs=(
            P("mem", "lat", "lon", None),
            P("lat", "lon", None),
            P("lat", "lon", None),
            P(None, ("lon", "lat"), None),
            P("mem", ("lon", "lat")),
            P("mem", ("lon", "lat"), None),
            P("mem", None, ("lon", "lat"), None),
        ),
        out_specs=P("mem", None, ("lon", "lat"), None),
        check_vma=False,
    )
```

```python
import functools

import jax
import jax.numpy as jnp
from jax import lax
from jax.experimental import pallas as pl
from jax.experimental.pallas import tpu as pltpu
from jax.sharding import PartitionSpec as P

MESH = pl.DeviceIdType.MESH
ZN, XN, YN = 8, 4, 4
PEERS = ZN * XN
ROWS = 32
MEMBERS = 1024
OBS = 512
BLK = 128
SLOTS = 4
SDIM = 1280
TILE = 256
STARTS = (4, 8, 14, 24)
PARTS = ((0, 896), (896, 384))


def kernel(
    ens_ref, innov_ref, wt_ref, loc_ref, cnt_ref, tap_ref, state_ref, out_ref,
    win0, win1, win2, win3, win4, win5, win6, win7, wside, pick, xfull, wgt, snat, spat, sfull, yroot, zroot, ynext, wmat, omat, obuf,
    ring_send, ring_recv, y_send, y_recv, side_send, side_recv,
    ens_send, ens_recv, st_send, st_recv, out_send, out_recv, nat_sem, loc_sem,
):
    wins = (win0, win1, win2, win3, win4, win5, win6, win7)
    me = lax.axis_index("mem")
    zc, xc = me // XN, me % XN
    yc = lax.axis_index("lon")
    sign = 1 - 2 * lax.axis_index("lat")

    def peer(dz, dx):
        return ((zc + dz) % ZN) * XN + (xc + dx) % XN

    def offset(k):
        lane = k % (ZN - 1)
        dz = (4 + 3 * (lane + lane // 4)) % ZN
        return dz, (k // (ZN - 1) + dz) % XN

    far = (ZN - 1) * XN
    y_up, y_down = (yc + 1) % YN, (yc + YN - 1) % YN

    group = 8
    natural = []
    for q in range(PEERS // group):
        copy = pltpu.make_async_copy(
            state_ref.at[:, pl.ds(q * group, group), :],
            snat.at[:, pl.ds(q * group, group), :], nat_sem.at[q],
        )
        copy.start()
        natural.append(copy)

    barrier = pltpu.get_barrier_semaphore()

    def greet(k, carry):
        dz, dx = offset(k)
        pl.semaphore_signal(
            barrier, inc=1, device_id={"mem": peer(dz, dx)}, device_id_type=MESH
        )
        return carry

    lax.fori_loop(0, far, greet, 0)
    for dx in range(1, XN):
        pl.semaphore_signal(
            barrier, inc=1, device_id={"mem": peer(0, dx)}, device_id_type=MESH
        )
    for other in (y_up, y_down):
        pl.semaphore_signal(barrier, inc=1, device_id={"lon": other}, device_id_type=MESH)

    wins[4][1] = jnp.swapaxes(ens_ref[...], 0, 1)
    wside[1, 0:16] = innov_ref[...].astype(jnp.float32)
    wside[1, 16:32] = wt_ref[...].astype(jnp.float32)
    pl.semaphore_wait(barrier, PEERS - 1 + 2)

    def unit(r):
        return (zc + sign * r + ZN) % ZN

    def ring_copy(arm, s):
        r = -s if arm == 0 else s
        r_there = r - 1 if arm == 0 else r + 1
        to = ((zc + sign * (1 - 2 * arm) + ZN) % ZN) * XN + xc
        i = arm * 4 + s
        return pltpu.make_async_remote_copy(
            src_ref=wins[r + 4].at[1], dst_ref=wins[r_there + 4].at[1],
            send_sem=ring_send.at[i], recv_sem=ring_recv.at[i],
            device_id={"mem": to}, device_id_type=MESH,
        )

    def y_copies(r):
        i = r + 4
        return [
            pltpu.make_async_remote_copy(
                src_ref=wins[i].at[1], dst_ref=wins[i].at[slot],
                send_sem=y_send.at[slot // 2, i], recv_sem=y_recv.at[slot // 2, i],
                device_id={"lon": other}, device_id_type=MESH,
            )
            for slot, other in ((0, y_up), (2, y_down))
        ]

    sides = [
        pltpu.make_async_remote_copy(
            src_ref=wside.at[1], dst_ref=wside.at[slot],
            send_sem=side_send.at[slot // 2], recv_sem=side_recv.at[slot // 2],
            device_id={"lon": other}, device_id_type=MESH,
        )
        for slot, other in ((0, y_up), (2, y_down))
    ]

    my_rows = pl.ds(pl.multiple_of(me * ROWS, ROWS), ROWS)

    def state_send(part, sem, dz, dx):
        to = peer(dz, dx)
        cols = pl.ds(*PARTS[part])
        return pltpu.make_async_remote_copy(
            src_ref=spat.at[to, :, cols], dst_ref=sfull.at[my_rows, cols],
            send_sem=st_send.at[part, sem], recv_sem=st_recv.at[part, sem],
            device_id={"mem": to}, device_id_type=MESH,
        )

    def state_copy(part):
        return lambda k: state_send(part, k, *offset(k))

    def start(make):
        def body(k, carry):
            make(k).start()
            return carry
        return body

    def wait_recv(make):
        def body(k, carry):
            make(k).wait_recv()
            return carry
        return body

    def wait_send(make):
        def body(k, carry):
            make(k).wait_send()
            return carry
        return body

    ring = {(0, 0): ring_copy(0, 0), (1, 0): ring_copy(1, 0)}
    rows_out = {0: y_copies(0)}
    for copy in list(ring.values()) + rows_out[0] + sides:
        copy.start()

    lanes = 128
    for q in range(PEERS // group):
        natural[q].wait()

        def relayout(t, carry):
            cols = pl.ds(pl.multiple_of(t * lanes, lanes), lanes)
            own = snat[:, q * group : (q + 1) * group, cols]
            spat[q * group : (q + 1) * group, :, cols] = jnp.swapaxes(own, 0, 1)
            return carry

        lax.fori_loop(0, SDIM // lanes, relayout, 0)

    own_state = pltpu.make_async_copy(spat.at[me], sfull.at[my_rows], loc_sem.at[0])
    own_state.start()
    near = [[state_send(h, far + dx - 1, 0, dx) for dx in range(1, XN)] for h in (0, 1)]
    for copy in near[0]:
        copy.start()

    done = 0
    for s in range(1, 5):
        for arm in (0, 1):
            if arm == 1 and s == 4:
                continue
            r = -s if arm == 0 else s
            ring[arm, s - 1].wait_recv()
            if s < 4 - arm:
                ring[arm, s] = ring_copy(arm, s)
                ring[arm, s].start()
            rows_out[r] = y_copies(r)
            for copy in rows_out[r]:
                copy.start()
        more = STARTS[s - 1]
        lax.fori_loop(done, more, start(state_copy(0)), 0)
        done = more

    def block_index(number):
        row = (number * 43) >> 9
        col = number - row * 12
        third = col >> 2
        return third, row * 4 + (col - third * 4)

    listed = [
        [block_index(loc_ref[j, zc * XN + (xc + dx) % XN]) for j in range(SLOTS)]
        for dx in range(XN)
    ]

    def full_rows(r, x):
        return pl.ds(pl.multiple_of((unit(r) * XN + x) * ROWS, ROWS), ROWS)

    def ens_copy(dx, r):
        i = r + 4
        return pltpu.make_async_remote_copy(
            src_ref=pick.at[dx - 1, i], dst_ref=xfull.at[full_rows(r, xc)],
            send_sem=ens_send.at[dx - 1, i], recv_sem=ens_recv.at[dx - 1, i],
            device_id={"mem": zc * XN + (xc + dx) % XN}, device_id_type=MESH,
        )

    picked = []
    for r in (0, -1, 1, -2, 2, -3, 3, -4):
        for copy in rows_out[r]:
            copy.wait_recv()
        for dx in (1, 2, 3, 0):
            for j in range(SLOTS):
                third, block = listed[dx][j]
                tile = wins[r + 4][third, block]
                cols = slice(j * BLK, (j + 1) * BLK)
                if dx:
                    pick[dx - 1, r + 4, :, cols] = tile
                else:
                    xfull[full_rows(r, xc), cols] = tile
            if dx:
                copy = ens_copy(dx, r)
                copy.start()
                picked.append(copy)
    lax.fori_loop(done, far, start(state_copy(0)), 0)
    for copy in near[1]:
        copy.start()
    lax.fori_loop(0, far, start(state_copy(1)), 0)
    for copy in sides:
        copy.wait_recv()

    count = cnt_ref[0]
    factors, innovs = [], []
    for j in range(SLOTS):
        third, block = listed[0][j]
        level = jnp.where(j < count, tap_ref[j], 0.0)
        innovs.append(wside[third, pl.ds(block, 1), :])
        factors.append(wside[third, pl.ds(block + 16, 1), :] * level)
    factor = jnp.concatenate(factors, axis=1)
    innov = jnp.concatenate(innovs, axis=1)

    for copy in picked:
        copy.wait_recv()

    drives = []
    total = jnp.zeros((1, 1), jnp.float32)
    for t in range(MEMBERS // TILE):
        rows = pl.ds(t * TILE, TILE)
        selected = xfull[rows, :].astype(jnp.float32)
        weighted = (selected * factor).astype(jnp.bfloat16)
        wgt[rows, :] = weighted
        weighted = weighted.astype(jnp.float32)
        drives.append(jnp.sum(weighted * innov, axis=1, keepdims=True))
        total += jnp.sum(
            jnp.sum(weighted * selected, axis=1, keepdims=True), axis=0, keepdims=True
        )
    divisor = float(MEMBERS - 1)
    level = 2.0 + total * (2.0 / (divisor * MEMBERS))
    inv_level = 1.0 / level
    inv_sqrt = 1.0 / jnp.sqrt(level)

    def eye(t):
        row = lax.broadcasted_iota(jnp.int32, (TILE, MEMBERS), 0) + t * TILE
        col = lax.broadcasted_iota(jnp.int32, (TILE, MEMBERS), 1)
        return jnp.where(row == col, 1.0, 0.0).astype(jnp.float32)

    def tile_rows(t):
        return pl.ds(pl.multiple_of(t * TILE, TILE), TILE)

    def gram_step(t, carry):
        rows = tile_rows(t)
        gram = lax.dot_general(
            wgt[rows, :], xfull[...], (((1,), (1,)), ((), ())),
            preferred_element_type=jnp.float32,
        )
        unit = eye(t)
        low = ((unit + gram * (1.0 / divisor)) * inv_level).astype(jnp.bfloat16)
        yroot[rows, :] = low
        zroot[rows, :] = (0.5 * (3.0 * unit - low.astype(jnp.float32))).astype(jnp.bfloat16)
        return carry

    lax.fori_loop(0, MEMBERS // TILE, gram_step, 0)

    def y_step(t, carry):
        rows = tile_rows(t)
        ynext[rows, :] = jnp.dot(
            yroot[rows, :], zroot[...], preferred_element_type=jnp.float32
        ).astype(jnp.bfloat16)
        return carry

    lax.fori_loop(0, MEMBERS // TILE, y_step, 0)

    def root_step(t, carry):
        rows = tile_rows(t)
        product = jnp.dot(zroot[rows, :], ynext[...], preferred_element_type=jnp.float32)
        half = (0.5 * (3.0 * eye(t) - product)).astype(jnp.bfloat16)
        last = jnp.dot(half, zroot[...], preferred_element_type=jnp.float32)
        yroot[rows, :] = (last * inv_sqrt).astype(jnp.bfloat16)
        return carry

    lax.fori_loop(0, MEMBERS // TILE, root_step, 0)

    drive = jnp.concatenate(drives, axis=0) * (1.0 / divisor)
    drive = jnp.broadcast_to(drive, (MEMBERS, BLK)).astype(jnp.bfloat16)
    inner = jnp.dot(yroot[...], drive, preferred_element_type=jnp.float32)
    mean = jnp.dot(yroot[...], inner.astype(jnp.bfloat16), preferred_element_type=jnp.float32)
    for t in range(MEMBERS // TILE):
        rows = pl.ds(t * TILE, TILE)
        full = yroot[rows, :].astype(jnp.float32) + mean[t * TILE : (t + 1) * TILE, 0:1]
        wmat[:, t * TILE : (t + 1) * TILE] = full.T.astype(jnp.bfloat16)

    def out_copy(part, k, dz, dx):
        to = peer(dz, dx)
        cols = pl.ds(*PARTS[part])
        return pltpu.make_async_remote_copy(
            src_ref=omat.at[pl.ds(pl.multiple_of(to * ROWS, ROWS), ROWS), cols],
            dst_ref=obuf.at[me, :, cols],
            send_sem=out_send.at[part, k], recv_sem=out_recv.at[part, k],
            device_id={"mem": to}, device_id_type=MESH,
        )

    own_state.wait()
    plane = XN * ROWS
    sends = []
    for part in (0, 1):
        cols = pl.ds(*PARTS[part])
        lax.fori_loop(0, far, wait_recv(state_copy(part)), 0)
        for copy in near[part]:
            copy.wait_recv()
        for pair in ((4, 7), (2, 5), (3, 6), (1, 0)):
            starts = [pl.multiple_of(((zc + dz) % ZN) * plane, plane) for dz in pair]
            left = jnp.concatenate([wmat[pl.ds(s, plane), :] for s in starts], axis=0)
            block = jnp.dot(left, sfull[:, cols], preferred_element_type=jnp.float32)
            block = block.astype(jnp.bfloat16)
            for i, s in enumerate(starts):
                omat[pl.ds(s, plane), cols] = block[i * plane : (i + 1) * plane, :]
            for turn in range(XN):
                for dz in pair:
                    dx = (turn + dz) % XN
                    if dz or dx:
                        copy = out_copy(part, dz * XN + dx, dz, dx)
                        copy.start()
                        sends.append(copy)
    obuf[me] = omat[my_rows, :]

    per_part = PEERS - 1
    for part in (0, 1):
        first, width = PARTS[part]
        for copy in sends[part * per_part : (part + 1) * per_part]:
            copy.wait_recv()
        for q in range(PEERS // group):
            pats = slice(q * group, (q + 1) * group)

            def restore(t, carry):
                cols = pl.ds(pl.multiple_of(first + t * lanes, lanes), lanes)
                out_ref[:, pats, cols] = jnp.swapaxes(obuf[pats, :, cols], 0, 1)
                return carry

            lax.fori_loop(0, width // lanes, restore, 0)

    lax.fori_loop(0, far, wait_send(state_copy(0)), 0)
    lax.fori_loop(0, far, wait_send(state_copy(1)), 0)
    early = list(ring.values()) + sides + near[0] + near[1] + picked
    for copies in rows_out.values():
        early += copies
    for copy in early + sends:
        copy.wait_send()


def on_device(ens_obs, innovation, obs_weight, loc_list, counts, taper, state):
    local, rows, cols, blk = ens_obs.shape
    blocks = rows * cols
    patches = loc_list.shape[0]
    vmem = pl.BlockSpec(memory_space=pltpu.VMEM)
    smem = pl.BlockSpec(memory_space=pltpu.SMEM)
    anywhere = pl.BlockSpec(memory_space=pl.ANY)
    dma = pltpu.SemaphoreType.DMA
    low = jnp.bfloat16
    out = pl.pallas_call(
        kernel,
        out_shape=pltpu.VMEM((local, patches, SDIM), low),
        in_specs=[
            vmem, vmem, vmem, smem, smem, smem,
            pl.BlockSpec(memory_space=pltpu.MemorySpace.HBM),
        ],
        out_specs=vmem,
        scratch_shapes=[
            *[pltpu.VMEM((3, blocks, local, blk), low)] * ZN,
            pltpu.VMEM((3, 2 * blocks, blk), jnp.float32),
            pltpu.VMEM((XN - 1, ZN, local, OBS), low),
            pltpu.VMEM((MEMBERS, OBS), low),
            pltpu.VMEM((MEMBERS, OBS), low),
            pltpu.VMEM((local, patches, SDIM), low),
            pltpu.VMEM((patches, local, SDIM), low),
            pltpu.VMEM((MEMBERS, SDIM), low),
            pltpu.VMEM((MEMBERS, MEMBERS), low),
            pltpu.VMEM((MEMBERS, MEMBERS), low),
            pltpu.VMEM((MEMBERS, MEMBERS), low),
            pltpu.VMEM((MEMBERS, MEMBERS), low),
            pltpu.VMEM((MEMBERS, SDIM), low),
            pltpu.VMEM((patches, local, SDIM), low),
            dma((7,)), dma((7,)), dma((2, ZN)), dma((2, ZN)), dma((2,)), dma((2,)),
            dma((XN - 1, ZN)), dma((XN - 1, ZN)), dma((2, PEERS - 1)), dma((2, PEERS - 1)),
            dma((2, PEERS)), dma((2, PEERS)), dma((4,)), dma((2,)),
        ],
        name="analysis",
        compiler_params=pltpu.CompilerParams(
            collective_id=0, has_side_effects=True, vmem_limit_bytes=56 << 20
        ),
    )(
        ens_obs.reshape(local, blocks, blk), innovation.reshape(blocks, blk),
        obs_weight.reshape(blocks, blk), jnp.transpose(loc_list, (2, 1, 0)).reshape(SLOTS, patches),
        counts.reshape(-1), taper.reshape(-1), state.reshape(local, patches, SDIM),
    )
    return out.reshape(local, patches, 1, SDIM)


def solution(mesh):
    return jax.shard_map(
        on_device,
        mesh=mesh,
        in_specs=(
            P("mem", "lat", "lon", None),
            P("lat", "lon", None),
            P("lat", "lon", None),
            P(None, ("lon", "lat"), None),
            P("mem", ("lon", "lat")),
            P("mem", ("lon", "lat"), None),
            P("mem", None, ("lon", "lat"), None),
        ),
        out_specs=P("mem", None, ("lon", "lat"), None),
        check_vma=False,
    )
```
